32 devices in a mesh: ctx: 2 (over core), ep: 16 (over z, y, x).
Axes of the slice: x: 2, y: 2, z: 4, core: 2. Of those that a mesh axis runs over, the one named last changes fastest.
Arguments:
- moe_rows: bfloat16 [1024, 3584], P('ep'), may hold values from -6 to 6
- routes: int32 [1024, 8], P('ep'), may hold values from 0 to 127, all different within a row; in each aligned block of 64 rows (0 to 63, 64 to 127, ...) at most 8 rows name the same one
- route_gates: float32 [1024, 8], P('ep'), may hold values from 0.1 to 1
- gate_weight: bfloat16 [128, 3584, 1024], P('ep', None, 'ctx'), may hold values from -0.09375 to 0.09375
- up_weight: bfloat16 [128, 3584, 1024], P('ep', None, 'ctx'), may hold values from -0.09375 to 0.09375
- down_weight: bfloat16 [128, 1024, 3584], P('ep', 'ctx'), may hold values from -0.1875 to 0.1875
- queries: bfloat16 [16, 64, 576], P('ep'), may hold values from -82 to 82
- latent_cache: bfloat16 [16, 4096, 576], P('ep', 'ctx'), may hold values from -6 to 6
- cache_lengths: int32 [16], P('ep'), may hold values from 128 to 4096, as said below
Outputs:
- routed_output: bfloat16 [1024, 3584], P('ep')
- attention_output: bfloat16 [16, 64, 512], P('ep', 'ctx')
The draws below stay inside these ranges and needn't reach their ends.
Inputs may be any that keep to these rules, and one draw needn't show every extreme that they name: `routes`: each row names 8 different experts. In each aligned block of 64 rows (the rows of one ep index) no expert is named by more than 8 rows, and in some blocks an expert is named by exactly 8 rows. `cache_lengths`: each length is a multiple of 128.
All inputs are finite; a program needn't handle non-finite values.
Results may differ from the reference program's by a relative error of at most 0.014.
Values may be sent and summed in bfloat16 or wider, within the bound.
No kernel may reach another device: no remote copies, remote signals or barrier semaphores. Data moves between devices by JAX's collectives and lax.ppermute only.
A program may use at most 256 MiB of HBM per device.

```python
import math
import jax
import jax.numpy as jnp
import numpy as np
from jax import lax

D = 3584
H = 64
LAT = 512
ROPE = 64
EXPERTS = 128
FFE = 1024
TOPK = 8
PAGE = 128
SEQS = 1
ROWS = 64
LMAX = 4096
CAP = 8
ROWS_ALL = 1024
SEQS_ALL = 16


def draw_queries(key, part):
    shape_all = (SEQS_ALL, H, LAT + ROPE)
    drawn = jnp.clip(jax.random.normal(jax.random.fold_in(key, 3), shape_all, jnp.float32), -6.0, 6.0)
    return drawn.astype(jnp.bfloat16)


def draw_latent_cache(key, part):
    shape_all = (SEQS_ALL, LMAX, LAT + ROPE)
    drawn = jnp.clip(jax.random.normal(jax.random.fold_in(key, 1), shape_all, jnp.float32), -6.0, 6.0)
    return drawn.astype(jnp.bfloat16)


def draw_cache_lengths(key, part):
    page_total = LMAX // PAGE
    pages = jax.random.randint(jax.random.fold_in(key, 4), (SEQS_ALL,), 1, page_total + 1, jnp.int32)
    longest = jax.random.randint(jax.random.fold_in(key, 5), (), 0, SEQS_ALL, jnp.int32)
    pages = jnp.where(jnp.arange(SEQS_ALL, dtype=jnp.int32) == longest, page_total, pages)
    return (pages * PAGE).astype(jnp.int32)


def levels(own_key, dims, split, low, high):
    loudness, own = 1.0, jax.random.fold_in(own_key, 6)
    for axis_at, shards_of in split:
        draws = jnp.exp(jax.random.uniform(jax.random.fold_in(own, axis_at), (shards_of,), jnp.float32, low / len(split), high / len(split)))
        loudness = loudness * jnp.repeat(draws, dims[axis_at] // shards_of).reshape([-1 if axis == axis_at else 1 for axis in range(len(dims))])
    return loudness


def shared_out(rng, own, number, rows, count, top, reach, skew):
    sequence = jax.random.permutation(rng, count)
    heavy_load, ordinary = load_shares(count, rows * top, reach, skew, True), load_shares(count, rows * top, reach, skew, False)
    places = jnp.arange(count)

    def named(sizes, offset_by):
        used = int((sizes > 0).sum())
        fixed = max(1, used // 4)
        passed = fixed + (places - fixed + offset_by * (used - fixed)) % max(1, count - fixed)
        return jnp.zeros((count,), jnp.int32).at[sequence[jnp.where(places < fixed, places, passed)]].set(jnp.asarray(sizes, jnp.int32))

    sizes = jnp.where(number % 4 == 0, named(heavy_load, number // 4), named(ordinary, number - number // 4 - 1))
    mixed = jax.random.permutation(jax.random.fold_in(own, 3), count)
    giver, sink = mixed[0:count // 2 * 2:2], mixed[1:count // 2 * 2:2]
    margin = jnp.minimum(sizes[giver] - 1, reach - sizes[sink]) // 2
    margin = jnp.where((giver == sequence[0]) | (sink == sequence[0]) | (sizes[sink] == 0), 0, jnp.maximum(margin, 0))
    passed = jax.random.randint(jax.random.fold_in(own, 4), (count // 2,), 0, 1 << 20) % (margin + 1)
    sizes = sizes.at[giver].add(-passed).at[sink].add(passed)
    items = jnp.searchsorted(jnp.cumsum(sizes), jnp.arange(rows * top), side="right").astype(jnp.int32)
    listing = items.reshape(top, rows).T
    listing = listing[jax.random.permutation(jax.random.fold_in(own, 1), rows)]
    offset_by = jax.random.randint(jax.random.fold_in(own, 2), (rows, 1), 0, top)
    return jnp.take_along_axis(listing, (jnp.arange(top)[None, :] + offset_by) % top, axis=1)


def load_shares(count, total, bound, slope, full):
    portions = [(1 << 20) // math.isqrt(grade ** slope) + 1 for grade in range(1, count + 1)]
    largest = bound if full else min(bound, max(-(-total // count), total * portions[0] // sum(portions)))
    least = 1 if total - largest >= count - 1 else 0
    counts, spare = [largest] + [least] * (count - 1), total - largest - least * (count - 1)
    while spare > 0:
        movable = [i for i in range(1, count) if counts[i] < largest] or [i for i in range(1, count) if counts[i] < bound]
        whole, left = sum([portions[i] for i in movable]), spare
        for i in movable:
            extra = min(bound - counts[i], max(1, left * portions[i] // whole), spare)
            counts[i] = counts[i] + extra
            spare = spare - extra
    return np.array(counts)


def bell_draw(key, dims, deviation, reach, pieces=(), kind=jnp.bfloat16):
    array = jax.random.normal(key, dims, jnp.float32) * deviation
    if len(pieces) > 0:
        array = levels(key, dims, pieces, -0.22, 0.18) * array
    return jnp.clip(array, min=-reach, max=reach).astype(kind)


def setup_inputs(seed: int = 0) -> dict:
    arg_keys = jax.random.split(jax.random.key(seed), 10)
    moe_rows = bell_draw(arg_keys[0], (ROWS_ALL, D), 1.0, 6.0, ((0, 16),))
    routes_keys = jax.random.split(jax.random.fold_in(arg_keys[1], 1), ROWS_ALL // ROWS)
    routes_turns = jax.random.permutation(jax.random.fold_in(arg_keys[1], 3), ROWS_ALL // ROWS)
    routes = jax.vmap(lambda own, number: shared_out(jax.random.fold_in(arg_keys[1], 2), own, number, ROWS, EXPERTS, TOPK, CAP, 2))(routes_keys, routes_turns).reshape((ROWS_ALL, TOPK))
    route_gates = jnp.clip(jnp.exp(math.log(1.0) - 2.3025851 * jax.random.uniform(arg_keys[2], (ROWS_ALL, TOPK), jnp.float32) ** levels(arg_keys[2], (ROWS_ALL, TOPK), ((0, 16),), -0.2, 0.2)), 0.1, 1.0)
    gate_weight = bell_draw(arg_keys[3], (EXPERTS, D, FFE), D ** -0.5, 0.09375, ((0, 16), (2, 2)))
    up_weight = bell_draw(arg_keys[4], (EXPERTS, D, FFE), D ** -0.5, 0.09375, ((0, 16), (2, 2)))
    down_weight = bell_draw(arg_keys[5], (EXPERTS, FFE, D), FFE ** -0.5, 0.1875, ((0, 16), (1, 2)))
    queries = draw_queries(jax.random.fold_in(arg_keys[9], 71), 0)
    latent_cache = draw_latent_cache(jax.random.fold_in(arg_keys[9], 71), 0)
    cache_lengths = draw_cache_lengths(jax.random.fold_in(arg_keys[9], 71), 0)
    return {"moe_rows": moe_rows, "routes": routes, "route_gates": route_gates, "gate_weight": gate_weight, "up_weight": up_weight, "down_weight": down_weight, "queries": queries, "latent_cache": latent_cache, "cache_lengths": cache_lengths}


softmax_scale = 192.0 ** -0.5


def expert_block(operands):
    inputs, gate_weight, up_weight, down_weight = operands
    gate_proj = jnp.dot(inputs, gate_weight, preferred_element_type=jnp.float32)
    up_proj = jnp.dot(inputs, up_weight, preferred_element_type=jnp.float32)
    hidden = (jax.nn.silu(gate_proj) * up_proj).astype(jnp.bfloat16)
    return jnp.dot(hidden, down_weight, preferred_element_type=jnp.float32).astype(jnp.bfloat16)


def attend_block(operands):
    queries, cache, lengths = operands
    scores = jnp.einsum('rhk,rlk->rhl', queries.astype(jnp.float32), cache.astype(jnp.float32)) * softmax_scale
    positions = jnp.arange(cache.shape[1], dtype=jnp.int32)
    usable = (positions[None, :] < lengths[:, None])[:, None, :]
    masked = jnp.where(usable, scores, -1e30)
    top_score = jnp.max(masked, axis=2, keepdims=True)
    weights = jnp.where(usable, jnp.exp(masked - top_score), 0.0)
    row_total = jnp.sum(weights, axis=2)
    rounded = lax.optimization_barrier(weights.astype(jnp.bfloat16)).astype(jnp.float32)
    values = jnp.einsum('rhl,rlv->rhv', rounded, cache[:, :, :LAT].astype(jnp.float32))
    return (values / row_total[:, :, None]).astype(jnp.bfloat16)


def reference(moe_rows, routes, route_gates, gate_weight, up_weight, down_weight, queries, latent_cache, cache_lengths):
    total_rows = moe_rows.shape[0]
    block_count = total_rows // ROWS
    pairs = routes.reshape(block_count, ROWS * TOPK)
    one_hot = (pairs[:, :, None] == jnp.arange(EXPERTS, dtype=jnp.int32)[None, None, :]).astype(jnp.int32)
    earlier = jnp.cumsum(one_hot, axis=1) - one_hot
    slots = jnp.sum(earlier * one_hot, axis=2).astype(jnp.int32)
    columns = (jnp.arange(block_count, dtype=jnp.int32)[:, None] * CAP + slots).reshape(-1).astype(jnp.int32)
    expert_ids = pairs.reshape(-1).astype(jnp.int32)
    row_ids = (jnp.arange(total_rows * TOPK, dtype=jnp.int32) // TOPK).astype(jnp.int32)
    buffers = jnp.zeros((EXPERTS, block_count * CAP, moe_rows.shape[1]), jnp.bfloat16)
    buffers = buffers.at[expert_ids, columns].set(moe_rows[row_ids])
    outputs = lax.map(expert_block, (buffers, gate_weight, up_weight, down_weight))
    picked = outputs[expert_ids, columns].astype(jnp.float32).reshape(total_rows, TOPK, moe_rows.shape[1])
    routed_output = jnp.sum(picked * route_gates[:, :, None], axis=1).astype(jnp.bfloat16)
    request_total = queries.shape[0]
    attend_count = request_total // SEQS
    attended = lax.map(attend_block, (queries.reshape(attend_count, SEQS, H, LAT + ROPE), latent_cache.reshape(attend_count, SEQS, LMAX, LAT + ROPE), cache_lengths.reshape(attend_count, SEQS)))
    return routed_output, attended.reshape(request_total, H, LAT)
```

```python
import functools

import jax
import jax.numpy as jnp
from jax import lax
from jax.experimental import pallas as pl
from jax.experimental.pallas import tpu as pltpu
from jax.sharding import PartitionSpec as P

LAT = 512
CAP = 8
JOIN = 4
COLS = 512

softmax_scale = 192.0 ** (-0.5)


def softmax_parts(queries, cache, cache_lengths, offset):
    local_span = cache.shape[1]
    scores = (
        jnp.einsum("rhk,rlk->rhl", queries, cache, preferred_element_type=jnp.float32)
        * softmax_scale
    )
    positions = offset + jnp.arange(local_span, dtype=jnp.int32)
    usable = (positions[None, :] < cache_lengths[:, None])[:, None, :]
    masked = jnp.where(usable, scores, -1e30)
    top_score = jnp.max(masked, axis=2)
    weights = jnp.where(usable, jnp.exp(masked - top_score[:, :, None]), 0.0)
    row_total = jnp.sum(weights, axis=2)
    values = jnp.einsum(
        "rhl,rlv->rhv",
        weights.astype(jnp.bfloat16),
        cache[:, :, :LAT],
        preferred_element_type=jnp.float32,
    )
    return (top_score, row_total, values)


def swap_ctx(x):
    return lax.ppermute(x, "ctx", [(0, 1), (1, 0)])


def attend_local(queries, latent_cache, cache_lengths):
    share = queries.shape[1] // 2
    mine = lax.axis_index("ctx")
    top, total, values = softmax_parts(
        queries, latent_cache, cache_lengths, mine * latent_cache.shape[1]
    )
    packed = jnp.concatenate(
        [values, jnp.stack([top, total], axis=2), jnp.zeros(top.shape + (126,), jnp.float32)],
        axis=2,
    )
    kept = lax.dynamic_slice_in_dim(packed, mine * share, share, 1)
    other = swap_ctx(lax.dynamic_slice_in_dim(packed, (1 - mine) * share, share, 1))
    kept_top, other_top = kept[:, :, LAT : LAT + 1], other[:, :, LAT : LAT + 1]
    joined_top = jnp.maximum(kept_top, other_top)
    kept_factor = jnp.exp(kept_top - joined_top)
    other_factor = jnp.exp(other_top - joined_top)
    joined = kept * kept_factor + other * other_factor
    return (joined[:, :, :LAT] / joined[:, :, LAT + 1 : LAT + 2]).astype(jnp.bfloat16)


def plane_of(owners):
    return owners == 16


def send(x, target):
    count = lax.axis_size("ep")
    return lax.ppermute(x, "ep", [(i, target(i)) for i in range(count)])


def to_x(x):
    return send(x, lambda i: i ^ 1)


def to_y(x):
    return send(x, lambda i: i ^ 2)


def to_z(x, steps):
    return send(x, lambda i: (i + 4 * steps) % 16)


def cat(*pieces):
    return jnp.concatenate(pieces, axis=0)


def after(x, other):
    return lax.optimization_barrier((x, other))[0]


def gather_rows(rows):
    n = rows.shape[0]
    h = n // 2
    below, above = to_z(rows, 1), to_z(rows, 3)
    own_x, own_y = to_x(rows), to_y(rows)
    far = to_z(after(rows, below), 2)
    bx = to_x(cat(below, above, own_y[h:]))
    by = to_y(cat(below, above, own_x[:h]))
    cx = to_x(cat(far, by[h:n], by[n + h : 2 * n]))
    cy = to_y(cat(far, bx[:h], bx[n : n + h]))
    dx = to_x(cy[h:n])
    dy = to_y(cx[:h])
    return [
        cat(rows, own_x, own_y, by[2 * n :], bx[2 * n :]),
        cat(below, bx[:n], by[:n], cy[n : n + h], cx[n : n + h]),
        cat(far, cx[:n], cy[:n], dy, dx),
        cat(above, bx[n : 2 * n], by[n : 2 * n], cy[n + h :], cx[n + h :]),
    ]


def scatter_sums(groups):
    n = groups[0].shape[0] // 4
    h = n // 2

    def part(k, j):
        return groups[k][j * n : (j + 1) * n]

    def plus(*terms):
        return sum(t.astype(jnp.float32) for t in terms).astype(jnp.bfloat16)

    dx = to_x(part(2, 3)[h:])
    dy = to_y(part(2, 3)[:h])
    far_x = cat(plus(part(2, 1)[:h], dy), part(2, 1)[h:])
    far_y = cat(part(2, 2)[:h], plus(part(2, 2)[h:], dx))
    cx = to_x(cat(far_x, part(1, 3)[h:], part(3, 3)[h:]))
    cy = to_y(cat(far_y, part(1, 3)[:h], part(3, 3)[:h]))
    far = to_z(plus(part(2, 0), cx[:n], cy[:n]), 2)
    bx = to_x(
        cat(
            plus(part(1, 1)[:h], cy[n : n + h]),
            part(1, 1)[h:],
            plus(part(3, 1)[:h], cy[n + h :]),
            part(3, 1)[h:],
            part(0, 3)[h:],
        )
    )
    by = to_y(
        cat(
            part(1, 2)[:h],
            plus(part(1, 2)[h:], cx[n : n + h]),
            part(3, 2)[:h],
            plus(part(3, 2)[h:], cx[n + h :]),
            part(0, 3)[:h],
        )
    )
    below = to_z(plus(part(1, 0), bx[:n], by[:n]), 3)
    above = to_z(plus(part(3, 0), bx[n : 2 * n], by[n : 2 * n]), 1)
    own_x = to_x(cat(plus(part(0, 1)[:h], by[2 * n :]), part(0, 1)[h:]))
    own_y = to_y(cat(part(0, 2)[:h], plus(part(0, 2)[h:], bx[2 * n :])))
    return plus(part(0, 0), own_x, own_y, below, above, far)


def expert_kernel(
    group_count,
    expert_count,
    first_ref,
    ids_ref,
    gates_ref,
    own_ref,
    other_ref,
    gate_ref,
    up_ref,
    down_ref,
    own_out,
    other_out,
    slots,
    results,
    select,
    scales,
):
    step = pl.program_id(0)
    half = own_ref.shape[0]
    lanes = 2 * half
    piece = half // JOIN
    block = JOIN * CAP
    width = own_ref.shape[1]

    @pl.when(step < group_count)
    def _():
        group = step
        first = first_ref[0]
        ids, gates = ids_ref[...], gates_ref[...]
        earlier = lax.broadcasted_iota(jnp.int32, (lanes, lanes), 0)
        later = lax.broadcasted_iota(jnp.int32, (lanes, lanes), 1)
        same = ((earlier // piece) % JOIN) == ((later // piece) % JOIN)
        before = jnp.where(same & (earlier < later), 1.0, 0.0).astype(jnp.bfloat16)
        named, gated = [], []
        for e in range(expert_count):
            hit = ids == (first + e).astype(jnp.float32)
            named.append(jnp.sum(jnp.where(hit, 1.0, 0.0), axis=0, keepdims=True))
            gated.append(jnp.sum(jnp.where(hit, gates, 0.0), axis=0, keepdims=True))
        padded = named + [jnp.zeros_like(named[0])] * (-expert_count % 8)
        places = jnp.dot(
            jnp.concatenate(padded, axis=0).astype(jnp.bfloat16),
            before,
            preferred_element_type=jnp.float32,
        )
        slot = lax.broadcasted_iota(jnp.int32, (block, lanes), 0)
        lane = lax.broadcasted_iota(jnp.int32, (block, lanes), 1)
        fits = (slot // CAP) == ((lane // piece) % JOIN)
        place = (slot % CAP).astype(jnp.float32)
        at = pl.ds(pl.multiple_of(group * block, block), block)
        for e in range(expert_count):
            wanted = jnp.where(named[e] > 0.5, places[e : e + 1], -1.0)
            picked = jnp.where(fits & (wanted == place), 1.0, 0.0)
            scale = jnp.sum(picked * gated[e], axis=1, keepdims=True)
            scales[e, at, :] = jnp.broadcast_to(scale, (block, 128))
            select[group, e * block : (e + 1) * block, :] = picked.astype(jnp.bfloat16)
        chosen = select[group]
        for c in range(0, width, COLS):
            rows = jnp.concatenate([own_ref[:, c : c + COLS], other_ref[:, c : c + COLS]], axis=0)
            sorted_rows = jnp.dot(chosen, rows, preferred_element_type=jnp.float32)
            for e in range(expert_count):
                slots[e, at, c : c + COLS] = sorted_rows[e * block : (e + 1) * block].astype(
                    jnp.bfloat16
                )

    @pl.when((step >= group_count) & (step < group_count + expert_count))
    def _():
        e = step - group_count
        rows = slots[e]
        gate = jnp.dot(rows, gate_ref[0], preferred_element_type=jnp.float32)
        up = jnp.dot(rows, up_ref[0], preferred_element_type=jnp.float32)
        hidden = (gate / (1.0 + jnp.exp(-gate))) * up * scales[e][:, :1]
        hidden = hidden.astype(jnp.bfloat16)
        for c in range(0, width, COLS):
            results[e, :, c : c + COLS] = jnp.dot(
                hidden, down_ref[0, :, c : c + COLS], preferred_element_type=jnp.float32
            ).astype(jnp.bfloat16)

    @pl.when(step >= group_count + expert_count)
    def _():
        group = step - group_count - expert_count
        chosen = select[group]
        at = pl.ds(pl.multiple_of(group * block, block), block)
        for c in range(0, width, COLS):
            outs = jnp.concatenate(
                [results[e, at, c : c + COLS] for e in range(expert_count)], axis=0
            )
            rows = lax.dot_general(
                chosen, outs, (((0,), (0,)), ((), ())), preferred_element_type=jnp.float32
            ).astype(jnp.bfloat16)
            own_out[:, c : c + COLS] = rows[:half]
            other_out[:, c : c + COLS] = rows[half:]


def expert_sums(own, other, ids, gates, first, gate_weight, up_weight, down_weight):
    expert_count, width, hidden = gate_weight.shape
    lanes = 8 * CAP * JOIN
    half = lanes // 2
    group_count = own.shape[0] // half
    slot_rows = group_count * JOIN * CAP

    def dealt(i, first_ref):
        return (jnp.minimum(i, group_count - 1), 0)

    def lane_block(i, first_ref):
        return (0, jnp.minimum(i, group_count - 1))

    def expert(i, first_ref):
        return (jnp.clip(i - group_count, 0, expert_count - 1), 0, 0)

    def summed(i, first_ref):
        return (jnp.maximum(i - group_count - expert_count, 0), 0)

    row_block = pl.BlockSpec((half, width), dealt)
    out_block = pl.BlockSpec((half, width), summed)
    weight_bytes = 3 * expert_count * width * hidden * 2
    return pl.pallas_call(
        functools.partial(expert_kernel, group_count, expert_count),
        out_shape=(jax.ShapeDtypeStruct(own.shape, jnp.bfloat16),) * 2,
        grid_spec=pltpu.PrefetchScalarGridSpec(
            num_scalar_prefetch=1,
            grid=(2 * group_count + expert_count,),
            in_specs=[
                pl.BlockSpec((ids.shape[0], lanes), lane_block),
                pl.BlockSpec((ids.shape[0], lanes), lane_block),
                row_block,
                row_block,
                pl.BlockSpec((1, width, hidden), expert),
                pl.BlockSpec((1, width, hidden), expert),
                pl.BlockSpec((1, hidden, width), expert),
            ],
            out_specs=[out_block, out_block],
            scratch_shapes=[
                pltpu.VMEM((expert_count, slot_rows, width), jnp.bfloat16),
                pltpu.VMEM((expert_count, slot_rows, width), jnp.bfloat16),
                pltpu.VMEM((group_count, expert_count * JOIN * CAP, lanes), jnp.bfloat16),
                pltpu.VMEM((expert_count, slot_rows, 128), jnp.float32),
            ],
        ),
        compiler_params=pltpu.CompilerParams(
            dimension_semantics=("arbitrary",), vmem_limit_bytes=56 * 1024 * 1024
        ),
        cost_estimate=pl.CostEstimate(
            flops=2 * slot_rows * weight_bytes // 2,
            bytes_accessed=weight_bytes,
            transcendentals=expert_count * slot_rows * hidden,
        ),
    )(first, ids, gates, own, other, gate_weight, up_weight, down_weight)


def route_rows(moe_rows, routes, route_gates, gate_weight, up_weight, down_weight):
    owners = lax.axis_size("ep")
    row_count, width = moe_rows.shape
    half = row_count // 2
    core, chip = lax.axis_index("ctx"), lax.axis_index("ep")
    local_experts = gate_weight.shape[0]
    group_count = owners // JOIN

    mine = lax.dynamic_slice_in_dim(moe_rows, core * half, half, 0)
    if plane_of(owners):
        own_groups = gather_rows(mine)
        other_groups = [swap_ctx(g) for g in own_groups]
        own, other = cat(*own_groups), cat(*other_groups)
        steps = jnp.arange(owners, dtype=jnp.int32)
        order = ((chip // 4 - steps // 4) % 4) * 4 + ((chip % 4) ^ (steps % 4))
    else:
        own = lax.all_gather(mine, "ep", tiled=True)
        other = swap_ctx(own)
        order = jnp.arange(owners, dtype=jnp.int32)

    named = jnp.concatenate([routes.astype(jnp.float32), route_gates], axis=1)
    named = lax.all_gather(named, "ep").reshape(owners, -1)
    placed = order[:, None] == jnp.arange(owners, dtype=jnp.int32)[None, :]
    named = jnp.sum(jnp.where(placed[:, :, None], named[None], 0.0), axis=1)
    named = named.reshape(group_count, JOIN, 2, half, -1)
    named = jnp.where(core == 0, named, named[:, :, ::-1])
    named = named.transpose(4, 0, 2, 1, 3).reshape(named.shape[-1], -1)
    top = routes.shape[1]
    first = (chip * local_experts).astype(jnp.int32).reshape(1)

    own_sums, other_sums = expert_sums(
        own, other, named[:top], named[top:], first, gate_weight, up_weight, down_weight
    )

    if plane_of(owners):
        rows = JOIN * half
        groups = [None] * group_count
        for k in (2, 1, 3, 0):
            at = slice(k * rows, (k + 1) * rows)
            groups[k] = own_sums[at] + swap_ctx(other_sums[at])
        own_final = scatter_sums(groups)
    else:
        both = own_sums + swap_ctx(other_sums)
        own_final = lax.psum_scatter(both, "ep", scatter_dimension=0, tiled=True)
    other_final = swap_ctx(own_final)
    return jnp.where(core == 0, cat(own_final, other_final), cat(other_final, own_final))


def body(
    moe_rows,
    routes,
    route_gates,
    gate_weight,
    up_weight,
    down_weight,
    queries,
    latent_cache,
    cache_lengths,
):
    routed_output = route_rows(moe_rows, routes, route_gates, gate_weight, up_weight, down_weight)
    attention_output = attend_local(queries, latent_cache, cache_lengths)
    return (routed_output, attention_output)


def solution(mesh):
    in_specs = (
        P("ep", None),
        P("ep", None),
        P("ep", None),
        P("ep", None, "ctx"),
        P("ep", None, "ctx"),
        P("ep", "ctx", None),
        P("ep", None, None),
        P("ep", "ctx", None),
        P("ep"),
    )
    out_specs = (P("ep", None), P("ep", "ctx", None))
    return jax.shard_map(body, mesh=mesh, in_specs=in_specs, out_specs=out_specs, check_vma=False)
```

```python
import functools

import jax
import jax.numpy as jnp
from jax import lax
from jax.experimental import pallas as pl
from jax.experimental.pallas import tpu as pltpu
from jax.sharding import PartitionSpec as P

LAT = 512
CAP = 8
JOIN = 4
COLS = 512

softmax_scale = 192.0 ** (-0.5)


def softmax_parts(queries, cache, cache_lengths, offset):
    local_span = cache.shape[1]
    scores = (
        jnp.einsum("rhk,rlk->rhl", queries, cache, preferred_element_type=jnp.float32)
        * softmax_scale
    )
    positions = offset + jnp.arange(local_span, dtype=jnp.int32)
    usable = (positions[None, :] < cache_lengths[:, None])[:, None, :]
    masked = jnp.where(usable, scores, -1e30)
    top_score = jnp.max(masked, axis=2)
    weights = jnp.where(usable, jnp.exp(masked - top_score[:, :, None]), 0.0)
    row_total = jnp.sum(weights, axis=2)
    values = jnp.einsum(
        "rhl,rlv->rhv",
        weights.astype(jnp.bfloat16),
        cache[:, :, :LAT],
        preferred_element_type=jnp.float32,
    )
    return (top_score, row_total, values)


def swap_ctx(x):
    return lax.ppermute(x, "ctx", [(0, 1), (1, 0)])


def attend_local(queries, latent_cache, cache_lengths):
    share = queries.shape[1] // 2
    mine = lax.axis_index("ctx")
    top, total, values = softmax_parts(
        queries, latent_cache, cache_lengths, mine * latent_cache.shape[1]
    )
    packed = jnp.concatenate(
        [values, jnp.stack([top, total], axis=2), jnp.zeros(top.shape + (126,), jnp.float32)],
        axis=2,
    )
    kept = lax.dynamic_slice_in_dim(packed, mine * share, share, 1)
    other = swap_ctx(lax.dynamic_slice_in_dim(packed, (1 - mine) * share, share, 1))
    kept_top, other_top = kept[:, :, LAT : LAT + 1], other[:, :, LAT : LAT + 1]
    joined_top = jnp.maximum(kept_top, other_top)
    kept_factor = jnp.exp(kept_top - joined_top)
    other_factor = jnp.exp(other_top - joined_top)
    joined = kept * kept_factor + other * other_factor
    return (joined[:, :, :LAT] / joined[:, :, LAT + 1 : LAT + 2]).astype(jnp.bfloat16)


def plane_of(owners):
    return owners == 16


def send(x, target):
    count = lax.axis_size("ep")
    return lax.ppermute(x, "ep", [(i, target(i)) for i in range(count)])


def to_x(x):
    return send(x, lambda i: i ^ 1)


def to_y(x):
    return send(x, lambda i: i ^ 2)


def to_z(x, steps):
    return send(x, lambda i: (i + 4 * steps) % 16)


def cat(*pieces):
    return jnp.concatenate(pieces, axis=0)


def after(x, other):
    return lax.optimization_barrier((x, other))[0]


def gather_rows(rows):
    n = rows.shape[0]
    h = n // 2
    below, above = to_z(rows, 1), to_z(rows, 3)
    own_x, own_y = to_x(rows), to_y(rows)
    far = to_z(after(rows, below), 2)
    bx = to_x(cat(below, above, own_y[h:]))
    by = to_y(cat(below, above, own_x[:h]))
    cx = to_x(cat(far, by[h:n], by[n + h : 2 * n]))
    cy = to_y(cat(far, bx[:h], bx[n : n + h]))
    dx = to_x(cy[h:n])
    dy = to_y(cx[:h])
    return (
        cat(rows, own_x, own_y, below, above),
        cat(bx, by),
        cat(far, cx, cy),
        cat(dx, dy),
    )


PLACES = (
    ((0, 0, 2), (0, 2, 4), (0, 4, 6), (1, 9, 10), (1, 4, 5)),
    ((0, 6, 8), (1, 0, 2), (1, 5, 7), (2, 8, 9), (2, 4, 5)),
    ((2, 0, 2), (2, 2, 4), (2, 6, 8), (3, 1, 2), (3, 0, 1)),
    ((0, 8, 10), (1, 2, 4), (1, 7, 9), (2, 9, 10), (2, 5, 6)),
)
BUNDLES = (10, 10, 10, 2)


def scatter_sums(kept, came):
    n = kept[3].shape[0]
    h = n // 2

    def share(b, first, last):
        at = slice(first * h, last * h)
        return kept[b][at].astype(jnp.float32) + came[b][at].astype(jnp.float32)

    def wide(x):
        return x.astype(jnp.float32)

    def narrow(*pieces):
        return cat(*pieces).astype(jnp.bfloat16)

    dx = wide(to_x(narrow(share(3, 0, 1))))
    dy = wide(to_y(narrow(share(3, 1, 2))))
    cx = wide(to_x(narrow(share(2, 2, 3) + dy, share(2, 3, 6))))
    cy = wide(to_y(narrow(share(2, 6, 7), share(2, 7, 8) + dx, share(2, 8, 10))))
    far = wide(to_z(narrow(share(2, 0, 2) + cx[:n] + cy[:n]), 2))
    bx = wide(
        to_x(
            narrow(
                share(1, 0, 1) + cy[n : n + h],
                share(1, 1, 2),
                share(1, 2, 3) + cy[n + h :],
                share(1, 3, 5),
            )
        )
    )
    by = wide(
        to_y(
            narrow(
                share(1, 5, 6),
                share(1, 6, 7) + cx[n : n + h],
                share(1, 7, 8),
                share(1, 8, 9) + cx[n + h :],
                share(1, 9, 10),
            )
        )
    )
    below = wide(to_z(narrow(share(0, 6, 8) + bx[:n] + by[:n]), 3))
    above = wide(to_z(narrow(share(0, 8, 10) + bx[n : 2 * n] + by[n : 2 * n]), 1))
    own_x = wide(to_x(narrow(share(0, 2, 3) + by[2 * n :], share(0, 3, 4))))
    own_y = wide(to_y(narrow(share(0, 4, 5), share(0, 5, 6) + bx[2 * n :])))
    return narrow(share(0, 0, 2) + own_x + own_y + below + above + far)


def expert_kernel(plan, first_ref, *refs):
    bundled, group_count, expert_count, width, top = plan
    count = len(BUNDLES) if bundled else 1
    own, other = refs[:count], refs[count : 2 * count]
    gate_ref, up_ref, down_ref = refs[2 * count : 2 * count + 3]
    own_out = refs[2 * count + 3 : 3 * count + 3]
    other_out = refs[3 * count + 3 : 4 * count + 3]
    slots, select, scales = refs[4 * count + 3 :]
    step = pl.program_id(0)
    lanes = select.shape[2]
    half = lanes // 2
    piece = half // JOIN
    block = JOIN * CAP
    unit = piece // 2

    def rows_of(group, at):
        parts = []
        for side in (own, other):
            if bundled:
                parts += [side[b][f * unit : t * unit, at] for b, f, t in PLACES[group]]
            else:
                parts.append(side[0][:, at])
        return jnp.concatenate(parts, axis=0)

    def put_rows(group, at, rows):
        done = 0
        for side in (own_out, other_out):
            if bundled:
                for b, f, t in PLACES[group]:
                    side[b][f * unit : t * unit, at] = rows[done : done + (t - f) * unit]
                    done += (t - f) * unit
            else:
                side[0][:, at] = rows[done : done + half]
                done += half

    def slot_range(group):
        if bundled:
            return slice(group * block, (group + 1) * block)
        return pl.ds(pl.multiple_of(group * block, block), block)

    def sort_rows(group):
        first = first_ref[0]
        named = rows_of(group, slice(width, width + 128)).astype(jnp.float32).T
        ids = named[:top]
        gates = named[top : 2 * top] + named[2 * top : 3 * top] + named[3 * top : 4 * top]
        earlier = lax.broadcasted_iota(jnp.int32, (lanes, lanes), 0)
        later = lax.broadcasted_iota(jnp.int32, (lanes, lanes), 1)
        same = ((earlier // piece) % JOIN) == ((later // piece) % JOIN)
        before = jnp.where(same & (earlier < later), 1.0, 0.0).astype(jnp.bfloat16)
        hits, gated = [], []
        for e in range(expert_count):
            hit = ids == (first + e).astype(jnp.float32)
            hits.append(jnp.sum(jnp.where(hit, 1.0, 0.0), axis=0, keepdims=True))
            gated.append(jnp.sum(jnp.where(hit, gates, 0.0), axis=0, keepdims=True))
        padded = hits + [jnp.zeros_like(hits[0])] * (-expert_count % 8)
        places = jnp.dot(
            jnp.concatenate(padded, axis=0).astype(jnp.bfloat16),
            before,
            preferred_element_type=jnp.float32,
        )
        slot = lax.broadcasted_iota(jnp.int32, (block, lanes), 0)
        lane = lax.broadcasted_iota(jnp.int32, (block, lanes), 1)
        fits = (slot // CAP) == ((lane // piece) % JOIN)
        place = (slot % CAP).astype(jnp.float32)
        at = slot_range(group)
        for e in range(expert_count):
            wanted = jnp.where(hits[e] > 0.5, places[e : e + 1], -1.0)
            picked = jnp.where(fits & (wanted == place), 1.0, 0.0)
            scale = jnp.sum(picked * gated[e], axis=1, keepdims=True)
            scales[e, at, :] = jnp.broadcast_to(scale, (block, 128))
            select[group, e * block : (e + 1) * block, :] = picked.astype(jnp.bfloat16)
        chosen = select[group]
        for c in range(0, width, COLS):
            columns = slice(c, c + COLS)
            sorted_rows = jnp.dot(
                chosen, rows_of(group, columns), preferred_element_type=jnp.float32
            ).astype(jnp.bfloat16)
            for e in range(expert_count):
                slots[e, at, columns] = sorted_rows[e * block : (e + 1) * block]

    def sum_rows(group):
        chosen = select[group]
        at = slot_range(group)
        for c in range(0, width, COLS):
            columns = slice(c, c + COLS)
            outs = jnp.concatenate([slots[e, at, columns] for e in range(expert_count)], axis=0)
            rows = lax.dot_general(
                chosen, outs, (((0,), (0,)), ((), ())), preferred_element_type=jnp.float32
            )
            put_rows(group, columns, rows.astype(jnp.bfloat16))

    def each_group(from_step, work):
        if bundled:
            for group in range(group_count):
                pl.when(step == from_step + group)(functools.partial(work, group))
        else:
            inside = (step >= from_step) & (step < from_step + group_count)
            pl.when(inside)(functools.partial(work, step - from_step))

    each_group(0, sort_rows)

    @pl.when((step >= group_count) & (step < group_count + expert_count))
    def _():
        e = step - group_count
        rows = slots[e]
        gate = jnp.dot(rows, gate_ref[0], preferred_element_type=jnp.float32)
        up = jnp.dot(rows, up_ref[0], preferred_element_type=jnp.float32)
        hidden = (gate / (1.0 + jnp.exp(-gate))) * up * scales[e][:, :1]
        hidden = hidden.astype(jnp.bfloat16)
        for c in range(0, width, COLS):
            slots[e, :, c : c + COLS] = jnp.dot(
                hidden, down_ref[0, :, c : c + COLS], preferred_element_type=jnp.float32
            ).astype(jnp.bfloat16)

    each_group(group_count + expert_count, sum_rows)


def expert_sums(own, other, top, owners, first, gate_weight, up_weight, down_weight):
    expert_count, width, hidden = gate_weight.shape
    bundled = len(own) > 1
    group_count = owners // JOIN
    half = sum(x.shape[0] for x in own) // group_count
    slot_rows = group_count * JOIN * CAP

    def expert(i, first_ref):
        return (jnp.clip(i - group_count, 0, expert_count - 1), 0, 0)

    if bundled:
        once = pl.Buffered(1)
        in_rows = [
            pl.BlockSpec(x.shape, lambda i, f: (0, 0), pipeline_mode=once) for x in own + other
        ]
        out_rows = [
            pl.BlockSpec((x.shape[0], width), lambda i, f: (0, 0), pipeline_mode=once)
            for x in own + other
        ]
    else:
        in_rows = [
            pl.BlockSpec((half, x.shape[1]), lambda i, f: (jnp.minimum(i, group_count - 1), 0))
            for x in own + other
        ]
        out_rows = [
            pl.BlockSpec((half, width), lambda i, f: (jnp.maximum(i - group_count - expert_count, 0), 0))
            for x in own + other
        ]
    weight_bytes = 3 * expert_count * width * hidden * 2
    sums = pl.pallas_call(
        functools.partial(
            expert_kernel, (bundled, group_count, expert_count, width, top)
        ),
        out_shape=[jax.ShapeDtypeStruct((x.shape[0], width), jnp.bfloat16) for x in own + other],
        grid_spec=pltpu.PrefetchScalarGridSpec(
            num_scalar_prefetch=1,
            grid=(2 * group_count + expert_count,),
            in_specs=in_rows
            + [
                pl.BlockSpec((1, width, hidden), expert),
                pl.BlockSpec((1, width, hidden), expert),
                pl.BlockSpec((1, hidden, width), expert),
            ],
            out_specs=out_rows,
            scratch_shapes=[
                pltpu.VMEM((expert_count, slot_rows, width), jnp.bfloat16),
                pltpu.VMEM((group_count, expert_count * JOIN * CAP, 2 * half), jnp.bfloat16),
                pltpu.VMEM((expert_count, slot_rows, 128), jnp.float32),
            ],
        ),
        compiler_params=pltpu.CompilerParams(
            dimension_semantics=("arbitrary",), vmem_limit_bytes=50 * 1024 * 1024
        ),
        cost_estimate=pl.CostEstimate(
            flops=slot_rows * weight_bytes,
            bytes_accessed=weight_bytes,
            transcendentals=expert_count * slot_rows * hidden,
        ),
    )(first, *own, *other, gate_weight, up_weight, down_weight)
    return sums[: len(own)], sums[len(own) :]


def as_three(x):
    terms = []
    for _ in range(3):
        term = lax.reduce_precision(x, 8, 7)
        terms.append(term.astype(jnp.bfloat16))
        x = x - term
    return terms


def route_rows(moe_rows, routes, route_gates, gate_weight, up_weight, down_weight):
    owners = lax.axis_size("ep")
    row_count = moe_rows.shape[0]
    top = routes.shape[1]
    half = row_count // 2
    core, chip = lax.axis_index("ctx"), lax.axis_index("ep")
    first = (chip * gate_weight.shape[0]).astype(jnp.int32).reshape(1)

    asked = [routes.astype(jnp.bfloat16)] + as_three(route_gates)
    blank = jnp.zeros((row_count, 128 - 4 * top), jnp.bfloat16)
    sent = jnp.concatenate([moe_rows] + asked + [blank], axis=1)
    sent = lax.dynamic_slice_in_dim(sent, core * half, half, 0)
    if plane_of(owners):
        own = gather_rows(sent)
    else:
        own = (lax.all_gather(sent, "ep", tiled=True),)
    other = tuple(swap_ctx(x) for x in own)
    own_sums, other_sums = expert_sums(
        own, other, top, owners, first, gate_weight, up_weight, down_weight
    )
    came = [None] * len(own)
    for b in reversed(range(len(own))):
        came[b] = swap_ctx(other_sums[b])
    if plane_of(owners):
        own_final = scatter_sums(own_sums, came)
    else:
        own_final = lax.psum_scatter(own_sums[0] + came[0], "ep", scatter_dimension=0, tiled=True)
    other_final = swap_ctx(own_final)
    return jnp.where(core == 0, cat(own_final, other_final), cat(other_final, own_final))


def body(
    moe_rows,
    routes,
    route_gates,
    gate_weight,
    up_weight,
    down_weight,
    queries,
    latent_cache,
    cache_lengths,
):
    routed_output = route_rows(moe_rows, routes, route_gates, gate_weight, up_weight, down_weight)
    attention_output = attend_local(queries, latent_cache, cache_lengths)
    return (routed_output, attention_output)


def solution(mesh):
    in_specs = (
        P("ep", None),
        P("ep", None),
        P("ep", None),
        P("ep", None, "ctx"),
        P("ep", None, "ctx"),
        P("ep", "ctx", None),
        P("ep", None, None),
        P("ep", "ctx", None),
        P("ep"),
    )
    out_specs = (P("ep", None), P("ep", "ctx", None))
    return jax.shard_map(body, mesh=mesh, in_specs=in_specs, out_specs=out_specs, check_vma=False)
```

```python
import functools

import jax
import jax.numpy as jnp
from jax import lax
from jax.experimental import pallas as pl
from jax.experimental.pallas import tpu as pltpu
from jax.sharding import PartitionSpec as P

LAT = 512
CAP = 8
JOIN = 4
COLS = 512
VMEM_LIMIT = 51 * 1024 * 1024

softmax_scale = 192.0 ** (-0.5)


def attend_kernel(span_ref, queries_ref, cache_ref, out_ref):
    heads, span = queries_ref.shape[0], cache_ref.shape[1]
    scores = (
        jnp.dot(queries_ref[...], cache_ref[...], preferred_element_type=jnp.float32)
        * softmax_scale
    )
    usable = lax.broadcasted_iota(jnp.int32, (heads, span), 1) < span_ref[0]
    masked = jnp.where(usable, scores, -1e30)
    top = jnp.max(masked, axis=1, keepdims=True)
    weights = jnp.where(usable, jnp.exp(masked - top), 0.0)
    total = jnp.sum(weights, axis=1, keepdims=True)
    out_ref[:, :LAT] = lax.dot_general(
        weights.astype(jnp.bfloat16),
        cache_ref[:LAT],
        (((1,), (1,)), ((), ())),
        preferred_element_type=jnp.float32,
    )
    lane = lax.broadcasted_iota(jnp.int32, (heads, 128), 1)
    out_ref[:, LAT:] = jnp.where(lane == 0, top, total)


def attend_part(queries, cache, span):
    heads, depth = queries.shape
    return pl.pallas_call(
        attend_kernel,
        out_shape=jax.ShapeDtypeStruct((heads, LAT + 128), jnp.float32),
        in_specs=[
            pl.BlockSpec(memory_space=pltpu.SMEM),
            pl.BlockSpec(memory_space=pltpu.VMEM),
            pl.BlockSpec(memory_space=pltpu.VMEM),
        ],
        out_specs=pl.BlockSpec(memory_space=pltpu.VMEM),
        compiler_params=pltpu.CompilerParams(vmem_limit_bytes=16 * 1024 * 1024),
        cost_estimate=pl.CostEstimate(
            flops=2 * heads * cache.shape[0] * (depth + LAT),
            bytes_accessed=cache.size * 2,
            transcendentals=heads * cache.shape[0],
        ),
    )(span, queries, cache.T)


def swap_ctx(x):
    return lax.ppermute(x, "ctx", [(0, 1), (1, 0)])


def attend_local(queries, latent_cache, cache_lengths):
    mine = lax.axis_index("ctx")
    spans = jnp.clip(
        cache_lengths - mine * latent_cache.shape[1], 0, latent_cache.shape[1]
    ).astype(jnp.int32)
    return jnp.stack(
        [
            attend_part(queries[r], latent_cache[r], spans[r : r + 1])
            for r in range(queries.shape[0])
        ]
    )


def join_cores(packed):
    mine, share = lax.axis_index("ctx"), packed.shape[1] // 2
    kept = lax.dynamic_slice_in_dim(packed, mine * share, share, 1)
    other = swap_ctx(lax.dynamic_slice_in_dim(packed, (1 - mine) * share, share, 1))
    kept_top, other_top = kept[:, :, LAT : LAT + 1], other[:, :, LAT : LAT + 1]
    joined_top = jnp.maximum(kept_top, other_top)
    kept_factor = jnp.exp(kept_top - joined_top)
    other_factor = jnp.exp(other_top - joined_top)
    joined = kept * kept_factor + other * other_factor
    return (joined[:, :, :LAT] / joined[:, :, LAT + 1 : LAT + 2]).astype(jnp.bfloat16)


def plane_of(owners):
    return owners == 16


def send(x, target):
    count = lax.axis_size("ep")
    return lax.ppermute(x, "ep", [(i, target(i)) for i in range(count)])


def to_x(x):
    return send(x, lambda i: i ^ 1)


def to_y(x):
    return send(x, lambda i: i ^ 2)


def to_z(x, steps):
    return send(x, lambda i: (i + 4 * steps) % 16)


def cat(*pieces):
    return jnp.concatenate(pieces, axis=0)


def after(x, other):
    return lax.optimization_barrier((x, other))[0]


def gather_rows(rows):
    n = rows.shape[0]
    h = n // 2
    below, above = to_z(rows, 1), to_z(rows, 3)
    own_x, own_y = to_x(rows), to_y(rows)
    far = to_z(after(rows, below), 2)
    bx = to_x(cat(below, above, own_y[h:]))
    by = to_y(cat(below, above, own_x[:h]))
    cx = to_x(cat(far, by[h:n], by[n + h : 2 * n]))
    cy = to_y(cat(far, bx[:h], bx[n : n + h]))
    dx = to_x(cy[h:n])
    dy = to_y(cx[:h])
    return [rows, own_x, own_y, below, above, bx, by, far, cx, cy, dx, dy]


TAKEN = (
    ((0, 0, 2), (1, 0, 2), (2, 0, 2), (6, 4, 5), (5, 4, 5)),
    ((3, 0, 2), (5, 0, 2), (6, 0, 2), (9, 2, 3), (8, 2, 3)),
    ((7, 0, 2), (8, 0, 2), (9, 0, 2), (11, 0, 1), (10, 0, 1)),
    ((4, 0, 2), (5, 2, 4), (6, 2, 4), (9, 3, 4), (8, 3, 4)),
)
OTHER = (
    ((0, 0, 2), (1, 0, 2), (1, 2, 4), (2, 9, 10), (2, 4, 5)),
    ((1, 4, 6), (2, 0, 2), (2, 5, 7), (3, 6, 7), (3, 2, 3)),
    ((2, 10, 12), (3, 0, 2), (3, 4, 6), (3, 9, 10), (3, 8, 9)),
    ((1, 6, 8), (2, 2, 4), (2, 7, 9), (3, 7, 8), (3, 3, 4)),
)
PLACES = (
    ((0, 0, 2), (0, 2, 4), (0, 4, 6), (1, 9, 10), (1, 4, 5)),
    ((0, 6, 8), (1, 0, 2), (1, 5, 7), (2, 8, 9), (2, 4, 5)),
    ((2, 0, 2), (2, 2, 4), (2, 6, 8), (3, 1, 2), (3, 0, 1)),
    ((0, 8, 10), (1, 2, 4), (1, 7, 9), (2, 9, 10), (2, 5, 6)),
)
BUNDLES = (10, 10, 10, 2)


def scatter_sums(kept, came):
    n = kept[3].shape[0]
    h = n // 2

    def share(b, first, last):
        at = slice(first * h, last * h)
        return kept[b][at].astype(jnp.float32) + came[b][at].astype(jnp.float32)

    def wide(x):
        return x.astype(jnp.float32)

    def narrow(*pieces):
        return cat(*pieces).astype(jnp.bfloat16)

    dx = wide(to_x(narrow(share(3, 0, 1))))
    dy = wide(to_y(narrow(share(3, 1, 2))))
    cx = wide(to_x(narrow(share(2, 2, 3) + dy, share(2, 3, 6))))
    cy = wide(to_y(narrow(share(2, 6, 7), share(2, 7, 8) + dx, share(2, 8, 10))))
    far = wide(to_z(narrow(share(2, 0, 2) + cx[:n] + cy[:n]), 2))
    bx = wide(
        to_x(
            narrow(
                share(1, 0, 1) + cy[n : n + h],
                share(1, 1, 2),
                share(1, 2, 3) + cy[n + h :],
                share(1, 3, 5),
            )
        )
    )
    by = wide(
        to_y(
            narrow(
                share(1, 5, 6),
                share(1, 6, 7) + cx[n : n + h],
                share(1, 7, 8),
                share(1, 8, 9) + cx[n + h :],
                share(1, 9, 10),
            )
        )
    )
    below = wide(to_z(narrow(share(0, 6, 8) + bx[:n] + by[:n]), 3))
    above = wide(to_z(narrow(share(0, 8, 10) + bx[n : 2 * n] + by[n : 2 * n]), 1))
    own_x = wide(to_x(narrow(share(0, 2, 3) + by[2 * n :], share(0, 3, 4))))
    own_y = wide(to_y(narrow(share(0, 4, 5), share(0, 5, 6) + bx[2 * n :])))
    return narrow(share(0, 0, 2) + own_x + own_y + below + above + far)


def expert_kernel(plan, first_ref, *refs):
    planes, group_count, expert_count, width, top = plan
    counts = (12, 4, 3) if planes else (1, 1, 3)
    counts += (4, 4) if planes else (1, 1)
    parts, done = [], 0
    for count in counts:
        parts.append(refs[done : done + count])
        done += count
    own, other, (gate_hbm, up_hbm, down_hbm), own_out, other_out = parts
    slots, select, scales, gate_buf, up_buf, down_buf, staged, sems, in_sems, out_sems = refs[done:]
    lanes = select.shape[2]
    half = lanes // 2
    piece = half // JOIN
    block = JOIN * CAP
    unit = piece // 2
    depth = gate_buf.shape[0]

    def loads(e):
        slot = lax.rem(e, depth)
        return [
            pltpu.make_async_copy(hbm.at[e], buf.at[slot], sems.at[k, slot])
            for k, (hbm, buf) in enumerate(
                ((gate_hbm, gate_buf), (up_hbm, up_buf), (down_hbm, down_buf))
            )
        ]

    def slot_range(group):
        if planes:
            return slice(group * block, (group + 1) * block)
        return pl.ds(pl.multiple_of(group * block, block), block)

    def block_of(group):
        return pl.ds(pl.multiple_of(group * half, half), half)

    def takes(group):
        if not planes:
            return [
                pltpu.make_async_copy(
                    ref[0].at[block_of(group)],
                    staged.at[0, pl.ds(k * half, half)],
                    in_sems.at[k],
                )
                for k, ref in enumerate((own, other))
            ]
        copies, at = [], 0
        for side, where in ((own, TAKEN), (other, OTHER)):
            for b, f, t in where[group]:
                rows = (t - f) * unit
                copies.append(
                    pltpu.make_async_copy(
                        side[b].at[pl.ds(f * unit, rows)],
                        staged.at[group, pl.ds(at, rows)],
                        in_sems.at[len(copies) + 10 * group],
                    )
                )
                at += rows
        return copies

    def puts(group):
        if not planes:
            return [
                pltpu.make_async_copy(
                    staged.at[0, pl.ds(k * half, half), pl.ds(0, width)],
                    ref[0].at[block_of(group)],
                    out_sems.at[k],
                )
                for k, ref in enumerate((own_out, other_out))
            ]
        copies, at = [], 0
        for side in (own_out, other_out):
            for b, f, t in PLACES[group]:
                rows = (t - f) * unit
                copies.append(
                    pltpu.make_async_copy(
                        staged.at[group, pl.ds(at, rows), pl.ds(0, width)],
                        side[b].at[pl.ds(f * unit, rows)],
                        out_sems.at[len(copies) + 10 * group],
                    )
                )
                at += rows
        return copies

    def stage_of(group):
        return group if planes else 0

    def sort_rows(group):
        copies = takes(group)
        if not planes:
            for copy in copies:
                copy.start()
        for copy in copies:
            copy.wait()
        rows_ref = staged.at[stage_of(group)]
        first = first_ref[0]
        named = rows_ref[:, width:].astype(jnp.float32).T
        ids = named[:top]
        gates = named[top : 2 * top] + named[2 * top : 3 * top] + named[3 * top : 4 * top]
        earlier = lax.broadcasted_iota(jnp.int32, (lanes, lanes), 0)
        later = lax.broadcasted_iota(jnp.int32, (lanes, lanes), 1)
        same = ((earlier // piece) % JOIN) == ((later // piece) % JOIN)
        before = jnp.where(same & (earlier < later), 1.0, 0.0).astype(jnp.bfloat16)
        hits, gated = [], []
        for e in range(expert_count):
            hit = ids == (first + e).astype(jnp.float32)
            hits.append(jnp.sum(jnp.where(hit, 1.0, 0.0), axis=0, keepdims=True))
            gated.append(jnp.sum(jnp.where(hit, gates, 0.0), axis=0, keepdims=True))
        padded = hits + [jnp.zeros_like(hits[0])] * (-expert_count % 8)
        places = jnp.dot(
            jnp.concatenate(padded, axis=0).astype(jnp.bfloat16),
            before,
            preferred_element_type=jnp.float32,
        )
        slot = lax.broadcasted_iota(jnp.int32, (block, lanes), 0)
        lane = lax.broadcasted_iota(jnp.int32, (block, lanes), 1)
        fits = (slot // CAP) == ((lane // piece) % JOIN)
        place = (slot % CAP).astype(jnp.float32)
        at = slot_range(group)
        for e in range(expert_count):
            wanted = jnp.where(hits[e] > 0.5, places[e : e + 1], -1.0)
            picked = jnp.where(fits & (wanted == place), 1.0, 0.0)
            scale = jnp.sum(picked * gated[e], axis=1, keepdims=True)
            scales[e, at, :] = jnp.broadcast_to(scale, (block, 128))
            select[group, e * block : (e + 1) * block, :] = picked.astype(jnp.bfloat16)
        chosen = select[group]
        for c in range(0, width, COLS):
            columns = slice(c, c + COLS)
            sorted_rows = jnp.dot(
                chosen, rows_ref[:, columns], preferred_element_type=jnp.float32
            ).astype(jnp.bfloat16)
            for e in range(expert_count):
                slots[e, at, columns] = sorted_rows[e * block : (e + 1) * block]

    def run_expert(e):
        slot = lax.rem(e, depth)
        gate_copy, up_copy, down_copy = loads(e)
        rows = slots[e]
        gate_copy.wait()
        gate = jnp.dot(rows, gate_buf[slot], preferred_element_type=jnp.float32)
        up_copy.wait()
        up = jnp.dot(rows, up_buf[slot], preferred_element_type=jnp.float32)
        hidden = (gate / (1.0 + jnp.exp(-gate))) * up * scales[e][:, :1]
        hidden = hidden.astype(jnp.bfloat16)
        down_copy.wait()
        for c in range(0, width, COLS):
            slots[e, :, c : c + COLS] = jnp.dot(
                hidden, down_buf[slot, :, c : c + COLS], preferred_element_type=jnp.float32
            ).astype(jnp.bfloat16)

        @pl.when(e + depth < expert_count)
        def _():
            for copy in loads(e + depth):
                copy.start()

    def sum_rows(group):
        chosen = select[group]
        at = slot_range(group)
        for c in range(0, width, COLS):
            columns = slice(c, c + COLS)
            outs = jnp.concatenate([slots[e, at, columns] for e in range(expert_count)], axis=0)
            rows = lax.dot_general(
                chosen, outs, (((0,), (0,)), ((), ())), preferred_element_type=jnp.float32
            )
            staged[stage_of(group), :, columns] = rows.astype(jnp.bfloat16)
        for copy in puts(group):
            copy.start()
        if not planes:
            for copy in puts(group):
                copy.wait()

    def each(count, work):
        lax.fori_loop(0, count, lambda i, _: (work(i), 0)[1], 0)

    if planes:
        for group in range(group_count):
            for copy in takes(group):
                copy.start()
    for e in range(min(depth, expert_count)):
        for copy in loads(e):
            copy.start()
    if planes:
        for group in range(group_count):
            sort_rows(group)
    else:
        each(group_count, sort_rows)
    each(expert_count, run_expert)
    if planes:
        for group in (2, 1, 3, 0):
            sum_rows(group)
        for group in (2, 1, 3, 0):
            for copy in puts(group):
                copy.wait()
    else:
        each(group_count, sum_rows)


def expert_sums(own, other, top, owners, first, gate_weight, up_weight, down_weight):
    expert_count, width, hidden = gate_weight.shape
    planes = plane_of(owners)
    group_count = owners // JOIN
    half = sum(x.shape[0] for x in own) // group_count
    slot_rows = group_count * JOIN * CAP
    depth = min(3, expert_count)
    if planes:
        out_rows = [u * half // 8 for u in BUNDLES] * 2
    else:
        out_rows = [own[0].shape[0]] * 2
    stages, copies = (group_count, 10 * group_count) if planes else (1, 2)
    weight_bytes = 3 * expert_count * width * hidden * 2
    sums = pl.pallas_call(
        functools.partial(expert_kernel, (planes, group_count, expert_count, width, top)),
        out_shape=[jax.ShapeDtypeStruct((r, width), jnp.bfloat16) for r in out_rows],
        in_specs=[pl.BlockSpec(memory_space=pltpu.SMEM)]
        + [pl.BlockSpec(memory_space=pl.ANY)] * (len(own) + len(other) + 3),
        out_specs=[pl.BlockSpec(memory_space=pl.ANY)] * len(out_rows),
        scratch_shapes=[
            pltpu.VMEM((expert_count, slot_rows, width), jnp.bfloat16),
            pltpu.VMEM((group_count, expert_count * JOIN * CAP, 2 * half), jnp.bfloat16),
            pltpu.VMEM((expert_count, slot_rows, 128), jnp.float32),
            pltpu.VMEM((depth, width, hidden), jnp.bfloat16),
            pltpu.VMEM((depth, width, hidden), jnp.bfloat16),
            pltpu.VMEM((depth, hidden, width), jnp.bfloat16),
            pltpu.VMEM((stages, 2 * half, own[0].shape[1]), jnp.bfloat16),
            pltpu.SemaphoreType.DMA((3, depth)),
            pltpu.SemaphoreType.DMA((copies,)),
            pltpu.SemaphoreType.DMA((copies,)),
        ],
        compiler_params=pltpu.CompilerParams(vmem_limit_bytes=VMEM_LIMIT),
        cost_estimate=pl.CostEstimate(
            flops=slot_rows * weight_bytes,
            bytes_accessed=weight_bytes,
            transcendentals=expert_count * slot_rows * hidden,
        ),
    )(first, *own, *other, gate_weight, up_weight, down_weight)
    return sums[: len(sums) // 2], sums[len(sums) // 2 :]


def ask_kernel(core_ref, rows_hbm, routes_hbm, gates_hbm, own_ref, other_ref, routes, gates, sems):
    width = rows_hbm.shape[1]
    half = rows_hbm.shape[0] // 2
    small = [
        pltpu.make_async_copy(routes_hbm, routes, sems.at[0]),
        pltpu.make_async_copy(gates_hbm, gates, sems.at[1]),
    ]
    large = [
        pltpu.make_async_copy(
            rows_hbm.at[pl.ds(pl.multiple_of(from_half * half, half), half)],
            ref.at[:, pl.ds(0, width)],
            sems.at[2 + k],
        )
        for k, (from_half, ref) in enumerate(
            ((core_ref[0], own_ref), (1 - core_ref[0], other_ref))
        )
    ]
    for copy in small + large:
        copy.start()
    for copy in small:
        copy.wait()
    terms = [routes[...].astype(jnp.float32)]
    left = gates[...]
    for _ in range(3):
        term = left.astype(jnp.bfloat16).astype(jnp.float32)
        terms.append(term)
        left = left - term
    blank = 128 - sum(t.shape[0] for t in terms)
    asked = jnp.concatenate(terms + [jnp.zeros((blank, 2 * half), jnp.float32)], axis=0).T
    asked = asked.astype(jnp.bfloat16)
    first, last = asked[:half], asked[half:]
    mine = core_ref[0] == 0
    own_ref[:, width:] = jnp.where(mine, first, last)
    other_ref[:, width:] = jnp.where(mine, last, first)
    for copy in large:
        copy.wait()


def ask(moe_rows, routes, route_gates, core):
    rows, width = moe_rows.shape
    half = jax.ShapeDtypeStruct((rows // 2, width + 128), jnp.bfloat16)
    return pl.pallas_call(
        ask_kernel,
        out_shape=(half, half),
        in_specs=[pl.BlockSpec(memory_space=pltpu.SMEM)]
        + [pl.BlockSpec(memory_space=pl.ANY)] * 3,
        out_specs=[pl.BlockSpec(memory_space=pltpu.VMEM)] * 2,
        scratch_shapes=[
            pltpu.VMEM(routes.shape[::-1], jnp.int32),
            pltpu.VMEM(routes.shape[::-1], jnp.float32),
            pltpu.SemaphoreType.DMA((4,)),
        ],
        compiler_params=pltpu.CompilerParams(vmem_limit_bytes=4 * 1024 * 1024),
    )(core.astype(jnp.int32).reshape(1), moe_rows, routes.T, route_gates.T)


def route_rows(moe_rows, routes, route_gates, gate_weight, up_weight, down_weight, packed):
    owners = lax.axis_size("ep")
    top = routes.shape[1]
    core, chip = lax.axis_index("ctx"), lax.axis_index("ep")
    first = (chip * gate_weight.shape[0]).astype(jnp.int32).reshape(1)

    mine, theirs = ask(moe_rows, routes, route_gates, core)
    if plane_of(owners):
        own = gather_rows(mine)
        other = [theirs] + [swap_ctx(cat(*x)) for x in (own[1:5], own[5:8], own[8:])]
    else:
        own = [lax.all_gather(mine, "ep", tiled=True)]
        other = [swap_ctx(own[0])]
    first, packed = lax.optimization_barrier((first, packed))
    own_sums, other_sums = expert_sums(
        own, other, top, owners, first, gate_weight, up_weight, down_weight
    )
    came = [None] * len(own_sums)
    for b in reversed(range(len(own_sums))):
        came[b] = swap_ctx(other_sums[b])
    if plane_of(owners):
        own_final = scatter_sums(own_sums, came)
    else:
        own_final = lax.psum_scatter(own_sums[0] + came[0], "ep", scatter_dimension=0, tiled=True)
    other_final = swap_ctx(own_final)
    routed = jnp.where(core == 0, cat(own_final, other_final), cat(other_final, own_final))
    return routed, packed


def body(
    moe_rows,
    routes,
    route_gates,
    gate_weight,
    up_weight,
    down_weight,
    queries,
    latent_cache,
    cache_lengths,
):
    packed = attend_local(queries, latent_cache, cache_lengths)
    routed_output, packed = route_rows(
        moe_rows, routes, route_gates, gate_weight, up_weight, down_weight, packed
    )
    return (routed_output, join_cores(packed))


def solution(mesh):
    in_specs = (
        P("ep", None),
        P("ep", None),
        P("ep", None),
        P("ep", None, "ctx"),
        P("ep", None, "ctx"),
        P("ep", "ctx", None),
        P("ep", None, None),
        P("ep", "ctx", None),
        P("ep"),
    )
    out_specs = (P("ep", None), P("ep", "ctx", None))
    return jax.shard_map(body, mesh=mesh, in_specs=in_specs, out_specs=out_specs, check_vma=False)
```

```python
import functools

import jax
import jax.numpy as jnp
from jax import lax
from jax.experimental import pallas as pl
from jax.experimental.pallas import tpu as pltpu
from jax.sharding import PartitionSpec as P

LAT = 512
CAP = 8
JOIN = 4
COLS = 512
AHEAD = 2
MORE = 2
VMEM_LIMIT = 71 * 512 * 1024

softmax_scale = 192.0 ** (-0.5)


def attend_kernel(request, here_ref, lengths_ref, queries_ref, cache_ref, kept_ref, sent_ref, joined):
    heads, span = queries_ref.shape[0], cache_ref.shape[1]
    share = heads // 2
    core = here_ref[0]
    scores = (
        jnp.dot(queries_ref[...], cache_ref[...], preferred_element_type=jnp.float32)
        * softmax_scale
    )
    positions = core * span + lax.broadcasted_iota(jnp.int32, (heads, span), 1)
    usable = positions < lengths_ref[request]
    masked = jnp.where(usable, scores, -1e30)
    top = jnp.max(masked, axis=1, keepdims=True)
    weights = jnp.where(usable, jnp.exp(masked - top), 0.0)
    total = jnp.sum(weights, axis=1, keepdims=True)
    joined[:, :LAT] = lax.dot_general(
        weights.astype(jnp.bfloat16),
        cache_ref[:LAT],
        (((1,), (1,)), ((), ())),
        preferred_element_type=jnp.float32,
    )
    lane = lax.broadcasted_iota(jnp.int32, (heads, 128), 1)
    joined[:, LAT:] = jnp.where(lane == 0, top, total)
    kept_ref[...] = joined[pl.ds(pl.multiple_of(core * share, share), share)]
    sent_ref[...] = joined[pl.ds(pl.multiple_of((1 - core) * share, share), share)]


def attend_part(queries, cache, lengths, request, here):
    heads, depth = queries.shape
    part = jax.ShapeDtypeStruct((heads // 2, LAT + 128), jnp.float32)
    return pl.pallas_call(
        functools.partial(attend_kernel, request),
        out_shape=(part, part),
        in_specs=[pl.BlockSpec(memory_space=pltpu.SMEM)] * 2
        + [pl.BlockSpec(memory_space=pltpu.VMEM)] * 2,
        out_specs=(pl.BlockSpec(memory_space=pltpu.VMEM),) * 2,
        scratch_shapes=[pltpu.VMEM((heads, LAT + 128), jnp.float32)],
        compiler_params=pltpu.CompilerParams(vmem_limit_bytes=16 * 1024 * 1024),
        cost_estimate=pl.CostEstimate(
            flops=2 * heads * cache.shape[0] * (depth + LAT),
            bytes_accessed=cache.size * 2,
            transcendentals=heads * cache.shape[0],
        ),
    )(here, lengths, queries, cache.T)


def swap_ctx(x):
    return lax.ppermute(x, "ctx", [(0, 1), (1, 0)])


def attend_local(queries, latent_cache, cache_lengths, here):
    parts = [
        attend_part(queries[r], latent_cache[r], cache_lengths, r, here)
        for r in range(queries.shape[0])
    ]
    return tuple(jnp.stack(half) for half in zip(*parts))


def join_cores(kept, sent):
    other = swap_ctx(sent)
    kept_top, other_top = kept[:, :, LAT : LAT + 1], other[:, :, LAT : LAT + 1]
    joined_top = jnp.maximum(kept_top, other_top)
    kept_factor = jnp.exp(kept_top - joined_top)
    other_factor = jnp.exp(other_top - joined_top)
    joined = kept * kept_factor + other * other_factor
    return (joined[:, :, :LAT] / joined[:, :, LAT + 1 : LAT + 2]).astype(jnp.bfloat16)


def plane_of(owners):
    return owners == 16


def send(x, target):
    count = lax.axis_size("ep")
    return lax.ppermute(x, "ep", [(i, target(i)) for i in range(count)])


def to_x(x):
    return send(x, lambda i: i ^ 1)


def to_y(x):
    return send(x, lambda i: i ^ 2)


def to_z(x, steps):
    return send(x, lambda i: (i + 4 * steps) % 16)


def cat(*pieces):
    return jnp.concatenate(pieces, axis=0)


def after(x, other):
    return lax.optimization_barrier((x, other))[0]


def gather_rows(rows, meanwhile):
    n = rows.shape[0]
    h = n // 2
    below, above = to_z(rows, 1), to_z(rows, 3)
    own_x, own_y = to_x(rows), to_y(rows)
    far = to_z(after(rows, below), 2)
    bx = to_x(cat(below, above, own_y[h:]))
    by = to_y(cat(below, above, own_x[:h]))
    early = swap_ctx(cat(own_x, own_y, below, above))
    result, done = meanwhile(above)
    far = far + done
    cx = to_x(cat(far, by[h:n], by[n + h : 2 * n]))
    cy = to_y(cat(far, bx[:h], bx[n : n + h]))
    middle = swap_ctx(cat(bx, by, far))
    dx = to_x(cy[h:n])
    dy = to_y(cx[:h])
    late = swap_ctx(cat(cx, cy))
    own = [rows, own_x, own_y, below, above, bx, by, far, cx, cy, dx, dy]
    return own, [early, middle, late, swap_ctx(cat(dx, dy))], result


TAKEN = (
    ((0, 0, 2), (1, 0, 2), (2, 0, 2), (6, 4, 5), (5, 4, 5)),
    ((3, 0, 2), (5, 0, 2), (6, 0, 2), (9, 2, 3), (8, 2, 3)),
    ((7, 0, 2), (8, 0, 2), (9, 0, 2), (11, 0, 1), (10, 0, 1)),
    ((4, 0, 2), (5, 2, 4), (6, 2, 4), (9, 3, 4), (8, 3, 4)),
)
OTHER = (
    ((0, 0, 2), (1, 0, 2), (1, 2, 4), (2, 9, 10), (2, 4, 5)),
    ((1, 4, 6), (2, 0, 2), (2, 5, 7), (3, 6, 7), (3, 2, 3)),
    ((2, 10, 12), (3, 0, 2), (3, 4, 6), (4, 1, 2), (4, 0, 1)),
    ((1, 6, 8), (2, 2, 4), (2, 7, 9), (3, 7, 8), (3, 3, 4)),
)
PLACES = (
    ((0, 0, 2), (0, 2, 4), (0, 4, 6), (1, 9, 10), (1, 4, 5)),
    ((0, 6, 8), (1, 0, 2), (1, 5, 7), (2, 8, 9), (2, 4, 5)),
    ((2, 0, 2), (2, 2, 4), (2, 6, 8), (3, 1, 2), (3, 0, 1)),
    ((0, 8, 10), (1, 2, 4), (1, 7, 9), (2, 9, 10), (2, 5, 6)),
)
BUNDLES = (10, 10, 10, 2)
ORDER = (2, 1, 3, 0)


def scatter_sums(kept, came):
    n = kept[3].shape[0]
    h = n // 2

    def share(b, first, last):
        at = slice(first * h, last * h)
        return kept[b][at].astype(jnp.float32) + came[b][at].astype(jnp.float32)

    def wide(x):
        return x.astype(jnp.float32)

    def narrow(*pieces):
        return cat(*pieces).astype(jnp.bfloat16)

    dx = wide(to_x(narrow(share(3, 0, 1))))
    dy = wide(to_y(narrow(share(3, 1, 2))))
    cx = wide(to_x(narrow(share(2, 2, 3) + dy, share(2, 3, 6))))
    cy = wide(to_y(narrow(share(2, 6, 7), share(2, 7, 8) + dx, share(2, 8, 10))))
    far = wide(to_z(narrow(share(2, 0, 2) + cx[:n] + cy[:n]), 2))
    bx = wide(
        to_x(
            narrow(
                share(1, 0, 1) + cy[n : n + h],
                share(1, 1, 2),
                share(1, 2, 3) + cy[n + h :],
                share(1, 3, 5),
            )
        )
    )
    by = wide(
        to_y(
            narrow(
                share(1, 5, 6),
                share(1, 6, 7) + cx[n : n + h],
                share(1, 7, 8),
                share(1, 8, 9) + cx[n + h :],
                share(1, 9, 10),
            )
        )
    )
    below = wide(to_z(narrow(share(0, 6, 8) + bx[:n] + by[:n]), 3))
    above = wide(to_z(narrow(share(0, 8, 10) + bx[n : 2 * n] + by[n : 2 * n]), 1))
    own_x = wide(to_x(narrow(share(0, 2, 3) + by[2 * n :], share(0, 3, 4))))
    own_y = wide(to_y(narrow(share(0, 4, 5), share(0, 5, 6) + bx[2 * n :])))
    others = lax.optimization_barrier(share(0, 0, 2) + below + above + far)
    return narrow(others + own_x + own_y)


def expert_kernel(plan, here_ref, *refs):
    planes, group_count, expert_count, width, top = plan
    counts = (12, 5, 3, 3) if planes else (1, 1, 3, 3)
    counts += (4, 4, 3) if planes else (1, 1, 3)
    parts, done = [], 0
    for count in counts:
        parts.append(refs[done : done + count])
        done += count
    own, other, (gate_hbm, up_hbm, down_hbm), _, own_out, other_out = parts[:6]
    gate_buf, up_buf, down_buf = parts[6]
    slots, select, scales, staged, sems, in_sems, out_sems, *room = refs[done:]
    sets = [[(ref, k) for ref in (gate_buf, up_buf, down_buf)] for k in range(gate_buf.shape[0])]
    if room:
        sets += [[(ref, k) for ref in room] for k in range(room[0].shape[0])]
    lanes = select.shape[2]
    half = lanes // 2
    piece = half // JOIN
    block = JOIN * CAP
    unit = piece // 2
    ahead, depth = gate_buf.shape[0], len(sets)

    def loads(e, slot):
        return [
            pltpu.make_async_copy(hbm.at[e], ref.at[k], sems.at[i, slot])
            for i, (hbm, (ref, k)) in enumerate(
                zip((gate_hbm, up_hbm, down_hbm), sets[slot], strict=True)
            )
        ]

    def slot_range(group):
        if planes:
            return slice(group * block, (group + 1) * block)
        return pl.ds(pl.multiple_of(group * block, block), block)

    def block_of(group):
        return pl.ds(pl.multiple_of(group * half, half), half)

    def takes(group):
        if not planes:
            return [
                pltpu.make_async_copy(
                    ref[0].at[block_of(group)],
                    staged.at[0, pl.ds(k * half, half)],
                    in_sems.at[k],
                )
                for k, ref in enumerate((own, other))
            ]
        copies, at = [], 0
        for side, where in ((own, TAKEN), (other, OTHER)):
            for b, f, t in where[group]:
                rows = (t - f) * unit
                copies.append(
                    pltpu.make_async_copy(
                        side[b].at[pl.ds(f * unit, rows)],
                        staged.at[stage_of(group), pl.ds(at, rows)],
                        in_sems.at[len(copies) + 10 * group],
                    )
                )
                at += rows
        return copies

    def puts(group):
        if not planes:
            return [
                pltpu.make_async_copy(
                    staged.at[0, pl.ds(k * half, half), pl.ds(0, width)],
                    ref[0].at[block_of(group)],
                    out_sems.at[k],
                )
                for k, ref in enumerate((own_out, other_out))
            ]
        copies, at = [], 0
        for side in (own_out, other_out):
            for b, f, t in PLACES[group]:
                rows = (t - f) * unit
                copies.append(
                    pltpu.make_async_copy(
                        staged.at[stage_of(group), pl.ds(at, rows), pl.ds(0, width)],
                        side[b].at[pl.ds(f * unit, rows)],
                        out_sems.at[len(copies) + 10 * group],
                    )
                )
                at += rows
        return copies

    def stage_of(group):
        return ORDER.index(group) % 2 if planes else 0

    def sort_rows(group):
        copies = takes(group)
        if not planes:
            for copy in copies:
                copy.start()
        for copy in copies:
            copy.wait()
        rows_ref = staged.at[stage_of(group)]
        first = here_ref[1]
        named = rows_ref[:, width:].astype(jnp.float32).T
        ids = named[:top]
        gates = named[top : 2 * top] + named[2 * top : 3 * top] + named[3 * top : 4 * top]
        earlier = lax.broadcasted_iota(jnp.int32, (lanes, lanes), 0)
        later = lax.broadcasted_iota(jnp.int32, (lanes, lanes), 1)
        same = ((earlier // piece) % JOIN) == ((later // piece) % JOIN)
        before = jnp.where(same & (earlier < later), 1.0, 0.0).astype(jnp.bfloat16)
        hits, gated = [], []
        for e in range(expert_count):
            hit = ids == (first + e).astype(jnp.float32)
            hits.append(jnp.sum(jnp.where(hit, 1.0, 0.0), axis=0, keepdims=True))
            gated.append(jnp.sum(jnp.where(hit, gates, 0.0), axis=0, keepdims=True))
        padded = hits + [jnp.zeros_like(hits[0])] * (-expert_count % 8)
        places = jnp.dot(
            jnp.concatenate(padded, axis=0).astype(jnp.bfloat16),
            before,
            preferred_element_type=jnp.float32,
        )
        slot = lax.broadcasted_iota(jnp.int32, (block, lanes), 0)
        lane = lax.broadcasted_iota(jnp.int32, (block, lanes), 1)
        fits = (slot // CAP) == ((lane // piece) % JOIN)
        place = (slot % CAP).astype(jnp.float32)
        at = slot_range(group)
        for e in range(expert_count):
            wanted = jnp.where(hits[e] > 0.5, places[e : e + 1], -1.0)
            picked = jnp.where(fits & (wanted == place), 1.0, 0.0)
            scale = jnp.sum(picked * gated[e], axis=1, keepdims=True)
            scales[e, at, :] = jnp.broadcast_to(scale, (block, 128))
            select[group, e * block : (e + 1) * block, :] = picked.astype(jnp.bfloat16)
        chosen = select[group]
        for c in range(0, width, COLS):
            columns = slice(c, c + COLS)
            sorted_rows = jnp.dot(
                chosen, rows_ref[:, columns], preferred_element_type=jnp.float32
            ).astype(jnp.bfloat16)
            for e in range(expert_count):
                slots[e, at, columns] = sorted_rows[e * block : (e + 1) * block]

    def run_expert(e, slot):
        copies = loads(e, slot)
        (gate_buf, k), (up_buf, _), (down_buf, _) = sets[slot]

        def arrived(copy):
            pl.when(e >= ahead)(copy.wait)

        def reload(i):
            @pl.when(e + depth < expert_count)
            def _():
                loads(e + depth, slot)[i].start()

        rows = slots[e]
        arrived(copies[0])
        gate = jnp.dot(rows, gate_buf[k], preferred_element_type=jnp.float32)
        reload(0)
        arrived(copies[1])
        up = jnp.dot(rows, up_buf[k], preferred_element_type=jnp.float32)
        reload(1)
        hidden = (gate / (1.0 + jnp.exp(-gate))) * up * scales[e][:, :1]
        hidden = hidden.astype(jnp.bfloat16)
        arrived(copies[2])
        for c in range(0, width, COLS):
            slots[e, :, c : c + COLS] = jnp.dot(
                hidden, down_buf[k, :, c : c + COLS], preferred_element_type=jnp.float32
            ).astype(jnp.bfloat16)

        reload(2)

    def run_experts(first):
        for slot in range(depth):
            run_expert(first * depth + slot, slot)

    def sum_rows(group):
        chosen = select[group]
        at = slot_range(group)
        for c in range(0, width, COLS):
            columns = slice(c, c + COLS)
            outs = jnp.concatenate([slots[e, at, columns] for e in range(expert_count)], axis=0)
            rows = lax.dot_general(
                chosen, outs, (((0,), (0,)), ((), ())), preferred_element_type=jnp.float32
            )
            staged[stage_of(group), :, columns] = rows.astype(jnp.bfloat16)
        for copy in puts(group):
            copy.start()
        if not planes:
            for copy in puts(group):
                copy.wait()

    def each(count, work):
        lax.fori_loop(0, count, lambda i, _: (work(i), 0)[1], 0)

    def start(copies):
        for copy in copies:
            copy.start()

    def wait(copies):
        for copy in copies:
            copy.wait()

    if planes:
        for group in ORDER[:2]:
            start(takes(group))
    for e in range(ahead, depth):
        start(loads(e, e))
    if planes:
        for place, group in enumerate(ORDER):
            sort_rows(group)
            if place + 2 < group_count:
                start(takes(ORDER[place + 2]))
    else:
        each(group_count, sort_rows)
    each(expert_count // depth, run_experts)
    if planes:
        for place, group in enumerate(ORDER):
            if place >= 2:
                wait(puts(ORDER[place - 2]))
            sum_rows(group)
        for group in ORDER[2:]:
            wait(puts(group))
    else:
        each(group_count, sum_rows)


def ahead_kernel(gate_hbm, up_hbm, down_hbm, _, __, gate_out, up_out, down_out, done_out, sems):
    copies = [
        pltpu.make_async_copy(hbm.at[e], out.at[e], sems.at[k, e])
        for e in range(gate_out.shape[0])
        for k, (hbm, out) in enumerate(
            ((gate_hbm, gate_out), (up_hbm, up_out), (down_hbm, down_out))
        )
    ]
    for copy in copies:
        copy.start()
    done_out[...] = jnp.zeros_like(done_out)
    for copy in copies:
        copy.wait()


def weights_ahead(gate_weight, up_weight, down_weight, *follows):
    depth = min(AHEAD, gate_weight.shape[0])
    assert gate_weight.shape[0] % depth == 0
    weights = [gate_weight, up_weight, down_weight]
    return pl.pallas_call(
        ahead_kernel,
        out_shape=[pltpu.VMEM((depth,) + w.shape[1:], w.dtype) for w in weights]
        + [jax.ShapeDtypeStruct(follows[0].shape, follows[0].dtype)],
        in_specs=[pl.BlockSpec(memory_space=pl.ANY)] * 5,
        out_specs=[pl.BlockSpec(memory_space=pltpu.VMEM)] * 4,
        scratch_shapes=[pltpu.SemaphoreType.DMA((3, depth))],
        compiler_params=pltpu.CompilerParams(vmem_limit_bytes=VMEM_LIMIT),
        cost_estimate=pl.CostEstimate(
            flops=0,
            bytes_accessed=sum(2 * depth * w[0].size for w in weights),
            transcendentals=0,
        ),
    )(*weights, *follows)


def expert_sums(own, other, top, owners, here, gate_weight, up_weight, down_weight, ahead):
    expert_count, width, hidden = gate_weight.shape
    planes = plane_of(owners)
    group_count = owners // JOIN
    half = sum(x.shape[0] for x in own) // group_count
    slot_rows = group_count * JOIN * CAP
    more = MORE if expert_count % (AHEAD + MORE) == 0 else 0
    depth = ahead[0].shape[0] + more
    ahead = [pltpu.with_memory_space_constraint(w, pltpu.VMEM) for w in ahead]
    if planes:
        out_rows = [u * half // 8 for u in BUNDLES] * 2
    else:
        out_rows = [own[0].shape[0]] * 2
    stages, copies = (2, 10 * group_count) if planes else (1, 2)
    weight_bytes = 3 * expert_count * width * hidden * 2
    sums = pl.pallas_call(
        functools.partial(expert_kernel, (planes, group_count, expert_count, width, top)),
        out_shape=[jax.ShapeDtypeStruct((r, width), jnp.bfloat16) for r in out_rows]
        + [pltpu.VMEM(w.shape, w.dtype) for w in ahead],
        input_output_aliases={
            1 + len(own) + len(other) + 3 + k: len(out_rows) + k for k in range(3)
        },
        in_specs=[pl.BlockSpec(memory_space=pltpu.SMEM)]
        + [pl.BlockSpec(memory_space=pl.ANY)] * (len(own) + len(other) + 3)
        + [pl.BlockSpec(memory_space=pltpu.VMEM)] * 3,
        out_specs=[pl.BlockSpec(memory_space=pl.ANY)] * len(out_rows)
        + [pl.BlockSpec(memory_space=pltpu.VMEM)] * 3,
        scratch_shapes=[
            pltpu.VMEM((expert_count, slot_rows, width), jnp.bfloat16),
            pltpu.VMEM((group_count, expert_count * JOIN * CAP, 2 * half), jnp.bfloat16),
            pltpu.VMEM((expert_count, slot_rows, 128), jnp.float32),
            pltpu.VMEM((stages, 2 * half, own[0].shape[1]), jnp.bfloat16),
            pltpu.SemaphoreType.DMA((3, depth)),
            pltpu.SemaphoreType.DMA((copies,)),
            pltpu.SemaphoreType.DMA((copies,)),
        ]
        + [pltpu.VMEM((more,) + w.shape[1:], w.dtype) for w in ahead if more],
        compiler_params=pltpu.CompilerParams(vmem_limit_bytes=VMEM_LIMIT),
        cost_estimate=pl.CostEstimate(
            flops=slot_rows * weight_bytes,
            bytes_accessed=weight_bytes,
            transcendentals=expert_count * slot_rows * hidden,
        ),
    )(here, *own, *other, gate_weight, up_weight, down_weight, *ahead)
    count = len(out_rows) // 2
    return sums[:count], sums[count : 2 * count]


def ask_kernel(here_ref, rows_hbm, routes_hbm, gates_hbm, own_ref, other_ref, routes, gates, asks, sems):
    width = rows_hbm.shape[1]
    half = rows_hbm.shape[0] // 2
    small = [
        pltpu.make_async_copy(routes_hbm, routes, sems.at[0]),
        pltpu.make_async_copy(gates_hbm, gates, sems.at[1]),
    ]
    large = [
        pltpu.make_async_copy(
            rows_hbm.at[pl.ds(pl.multiple_of(from_half * half, half), half)],
            ref.at[:, pl.ds(0, width)],
            sems.at[2 + k],
        )
        for k, (from_half, ref) in enumerate(
            ((here_ref[0], own_ref), (1 - here_ref[0], other_ref))
        )
    ]
    for copy in small + large:
        copy.start()
    for copy in small:
        copy.wait()
    terms = [routes[...].astype(jnp.float32)]
    left = gates[...]
    for _ in range(3):
        term = left.astype(jnp.bfloat16).astype(jnp.float32)
        terms.append(term)
        left = left - term
    blank = 128 - sum(t.shape[0] for t in terms)
    asked = jnp.concatenate(terms + [jnp.zeros((blank, 2 * half), jnp.float32)], axis=0).T
    asked = asked.astype(jnp.bfloat16)
    first, last = asked[:half], asked[half:]
    mine = here_ref[0] == 0
    own_ref[:, width:] = jnp.where(mine, first, last)
    asks[...] = jnp.where(mine, last, first)
    last = pltpu.make_async_copy(asks, other_ref.at[:, pl.ds(width, 128)], sems.at[4])
    last.start()
    for copy in large + [last]:
        copy.wait()


def ask(moe_rows, routes, route_gates, here):
    rows, width = moe_rows.shape
    half = jax.ShapeDtypeStruct((rows // 2, width + 128), jnp.bfloat16)
    return pl.pallas_call(
        ask_kernel,
        out_shape=(half, half),
        in_specs=[pl.BlockSpec(memory_space=pltpu.SMEM)]
        + [pl.BlockSpec(memory_space=pl.ANY)] * 3,
        out_specs=[pl.BlockSpec(memory_space=pltpu.VMEM), pl.BlockSpec(memory_space=pl.ANY)],
        scratch_shapes=[
            pltpu.VMEM(routes.shape[::-1], jnp.int32),
            pltpu.VMEM(routes.shape[::-1], jnp.float32),
            pltpu.VMEM((rows // 2, 128), jnp.bfloat16),
            pltpu.SemaphoreType.DMA((5,)),
        ],
        compiler_params=pltpu.CompilerParams(vmem_limit_bytes=4 * 1024 * 1024),
    )(
        here,
        *(pltpu.with_memory_space_constraint(x, pltpu.HBM) for x in (moe_rows, routes.T, route_gates.T)),
    )


def order_kernel(here_ref, own_ref, other_ref, out_ref):
    half = own_ref.shape[0]
    out_ref[pl.ds(pl.multiple_of(here_ref[0] * half, half), half)] = own_ref[...]
    out_ref[pl.ds(pl.multiple_of((1 - here_ref[0]) * half, half), half)] = other_ref[...]


def in_order(own, other, here):
    return pl.pallas_call(
        order_kernel,
        out_shape=jax.ShapeDtypeStruct((2 * own.shape[0], own.shape[1]), own.dtype),
        in_specs=[pl.BlockSpec(memory_space=pltpu.SMEM)]
        + [pl.BlockSpec(memory_space=pltpu.VMEM)] * 2,
        out_specs=pl.BlockSpec(memory_space=pltpu.VMEM),
        compiler_params=pltpu.CompilerParams(vmem_limit_bytes=4 * 1024 * 1024),
    )(here, own, other)


def route_rows(moe_rows, routes, route_gates, gate_weight, up_weight, down_weight, attend):
    owners = lax.axis_size("ep")
    top = routes.shape[1]
    core, chip = lax.axis_index("ctx"), lax.axis_index("ep")
    here = jnp.stack([core, chip * gate_weight.shape[0]]).astype(jnp.int32)

    def meanwhile(follows):
        packed = attend(here)
        *ahead, done = weights_ahead(gate_weight, up_weight, down_weight, follows, packed[0])
        return (ahead, packed), done

    mine, theirs = ask(moe_rows, routes, route_gates, here)
    if plane_of(owners):
        own, other, (ahead, packed) = gather_rows(mine, meanwhile)
        other = [theirs] + other
    else:
        own = [lax.all_gather(mine, "ep", tiled=True)]
        other = [swap_ctx(own[0])]
        ahead, packed = meanwhile(mine)[0]
    own_sums, other_sums = expert_sums(
        own, other, top, owners, here, gate_weight, up_weight, down_weight, ahead
    )
    came = [None] * len(own_sums)
    for b in reversed(range(len(own_sums))):
        came[b] = swap_ctx(other_sums[b])
    if plane_of(owners):
        own_final = scatter_sums(own_sums, came)
    else:
        own_final = lax.psum_scatter(own_sums[0] + came[0], "ep", scatter_dimension=0, tiled=True)
    other_final = swap_ctx(own_final)
    return in_order(own_final, other_final, here), packed


def body(
    moe_rows,
    routes,
    route_gates,
    gate_weight,
    up_weight,
    down_weight,
    queries,
    latent_cache,
    cache_lengths,
):
    attend = functools.partial(attend_local, queries, latent_cache, cache_lengths)
    routed_output, packed = route_rows(
        moe_rows, routes, route_gates, gate_weight, up_weight, down_weight, attend
    )
    return (routed_output, join_cores(*packed))


def solution(mesh):
    in_specs = (
        P("ep", None),
        P("ep", None),
        P("ep", None),
        P("ep", None, "ctx"),
        P("ep", None, "ctx"),
        P("ep", "ctx", None),
        P("ep", None, None),
        P("ep", "ctx", None),
        P("ep"),
    )
    out_specs = (P("ep", None), P("ep", "ctx", None))
    return jax.shard_map(body, mesh=mesh, in_specs=in_specs, out_specs=out_specs, check_vma=False)
```

```python
import functools

import jax
import jax.numpy as jnp
from jax import lax
from jax.experimental import pallas as pl
from jax.experimental.pallas import tpu as pltpu
from jax.sharding import PartitionSpec as P

LAT = 512
CAP = 8
JOIN = 4
COLS = 512
AHEAD = 3
MORE = 1
VMEM_LIMIT = 55 * 512 * 1024

softmax_scale = 192.0 ** (-0.5)


def attend_kernel(request, here_ref, lengths_ref, queries_ref, cache_ref, kept_ref, sent_ref, zeros_ref, joined):
    zeros_ref[...] = jnp.zeros_like(zeros_ref)
    heads, span = queries_ref.shape[0], cache_ref.shape[1]
    share = heads // 2
    core = here_ref[0]
    scores = (
        jnp.dot(queries_ref[...], cache_ref[...], preferred_element_type=jnp.float32)
        * softmax_scale
    )
    positions = core * span + lax.broadcasted_iota(jnp.int32, (heads, span), 1)
    usable = positions < lengths_ref[request]
    masked = jnp.where(usable, scores, -1e30)
    top = jnp.max(masked, axis=1, keepdims=True)
    weights = jnp.where(usable, jnp.exp(masked - top), 0.0)
    total = jnp.sum(weights, axis=1, keepdims=True)
    joined[:, :LAT] = lax.dot_general(
        weights.astype(jnp.bfloat16),
        cache_ref[:LAT],
        (((1,), (1,)), ((), ())),
        preferred_element_type=jnp.float32,
    )
    lane = lax.broadcasted_iota(jnp.int32, (heads, 128), 1)
    joined[:, LAT:] = jnp.where(lane == 0, top, total)
    kept_ref[...] = joined[pl.ds(pl.multiple_of(core * share, share), share)]
    sent_ref[...] = joined[pl.ds(pl.multiple_of((1 - core) * share, share), share)]


def attend_part(queries, cache, lengths, request, here, like):
    heads, depth = queries.shape
    part = jax.ShapeDtypeStruct((heads // 2, LAT + 128), jnp.float32)
    return pl.pallas_call(
        functools.partial(attend_kernel, request),
        out_shape=(part, part, jax.ShapeDtypeStruct(like.shape, like.dtype)),
        in_specs=[pl.BlockSpec(memory_space=pltpu.SMEM)] * 2
        + [pl.BlockSpec(memory_space=pltpu.VMEM)] * 2,
        out_specs=(pl.BlockSpec(memory_space=pltpu.VMEM),) * 3,
        scratch_shapes=[pltpu.VMEM((heads, LAT + 128), jnp.float32)],
        compiler_params=pltpu.CompilerParams(vmem_limit_bytes=16 * 1024 * 1024),
        cost_estimate=pl.CostEstimate(
            flops=2 * heads * cache.shape[0] * (depth + LAT),
            bytes_accessed=cache.size * 2,
            transcendentals=heads * cache.shape[0],
        ),
    )(here, lengths, queries, cache.T)


def swap_ctx(x):
    return lax.ppermute(x, "ctx", [(0, 1), (1, 0)])


def attend_local(queries, latent_cache, cache_lengths, here, like):
    parts = [
        attend_part(queries[r], latent_cache[r], cache_lengths, r, here, like)
        for r in range(queries.shape[0])
    ]
    kept, sent, zeros = zip(*parts)
    return (jnp.stack(kept), jnp.stack(sent)), zeros[-1]


def join_cores(kept, sent):
    other = swap_ctx(sent)
    kept_top, other_top = kept[:, :, LAT : LAT + 1], other[:, :, LAT : LAT + 1]
    joined_top = jnp.maximum(kept_top, other_top)
    kept_factor = jnp.exp(kept_top - joined_top)
    other_factor = jnp.exp(other_top - joined_top)
    joined = kept * kept_factor + other * other_factor
    return (joined[:, :, :LAT] / joined[:, :, LAT + 1 : LAT + 2]).astype(jnp.bfloat16)


def plane_of(owners):
    return owners == 16


def send(x, target):
    count = lax.axis_size("ep")
    return lax.ppermute(x, "ep", [(i, target(i)) for i in range(count)])


def to_x(x):
    return send(x, lambda i: i ^ 1)


def to_y(x):
    return send(x, lambda i: i ^ 2)


def to_z(x, steps):
    return send(x, lambda i: (i + 4 * steps) % 16)


def cat(*pieces):
    return jnp.concatenate(pieces, axis=0)


def after(x, other):
    return lax.optimization_barrier((x, other))[0]


def gather_rows(rows, meanwhile):
    n = rows.shape[0]
    h = n // 2
    below, above = to_z(rows, 1), to_z(rows, 3)
    own_x, own_y = to_x(rows), to_y(rows)
    far = to_z(after(rows, below), 2)
    result, begun, done = meanwhile(above)
    bx = to_x(cat(below, above + begun, own_y[h:]))
    by = to_y(cat(below, above + begun, own_x[:h]))
    early = swap_ctx(cat(own_x, own_y, below, above))
    far = far + done
    cx = to_x(cat(far, by[h:n], by[n + h : 2 * n]))
    cy = to_y(cat(far, bx[:h], bx[n : n + h]))
    middle = swap_ctx(cat(bx, by, far))
    dx = to_x(cy[h:n])
    dy = to_y(cx[:h])
    late = swap_ctx(cat(cx, cy))
    own = [rows, own_x, own_y, below, above, bx, by, far, cx, cy, dx, dy]
    return own, [early, middle, late, swap_ctx(cat(dx, dy))], result


TAKEN = (
    ((0, 0, 2), (1, 0, 2), (2, 0, 2), (6, 4, 5), (5, 4, 5)),
    ((3, 0, 2), (5, 0, 2), (6, 0, 2), (9, 2, 3), (8, 2, 3)),
    ((7, 0, 2), (8, 0, 2), (9, 0, 2), (11, 0, 1), (10, 0, 1)),
    ((4, 0, 2), (5, 2, 4), (6, 2, 4), (9, 3, 4), (8, 3, 4)),
)
OTHER = (
    ((0, 0, 2), (1, 0, 2), (1, 2, 4), (2, 9, 10), (2, 4, 5)),
    ((1, 4, 6), (2, 0, 2), (2, 5, 7), (3, 6, 7), (3, 2, 3)),
    ((2, 10, 12), (3, 0, 2), (3, 4, 6), (4, 1, 2), (4, 0, 1)),
    ((1, 6, 8), (2, 2, 4), (2, 7, 9), (3, 7, 8), (3, 3, 4)),
)
PLACES = (
    ((0, 0, 2), (0, 2, 4), (0, 4, 6), (1, 9, 10), (1, 4, 5)),
    ((0, 6, 8), (1, 0, 2), (1, 5, 7), (2, 8, 9), (2, 4, 5)),
    ((2, 0, 2), (2, 2, 4), (2, 6, 8), (3, 1, 2), (3, 0, 1)),
    ((0, 8, 10), (1, 2, 4), (1, 7, 9), (2, 9, 10), (2, 5, 6)),
)
BUNDLES = (10, 10, 10, 2)


def scatter_sums(kept, came):
    n = kept[3].shape[0]
    h = n // 2

    def share(b, first, last):
        at = slice(first * h, last * h)
        return kept[b][at].astype(jnp.float32) + came[b][at].astype(jnp.float32)

    def wide(x):
        return x.astype(jnp.float32)

    def narrow(*pieces):
        return cat(*pieces).astype(jnp.bfloat16)

    dx = wide(to_x(narrow(share(3, 0, 1))))
    dy = wide(to_y(narrow(share(3, 1, 2))))
    cx = wide(to_x(narrow(share(2, 2, 3) + dy, share(2, 3, 6))))
    cy = wide(to_y(narrow(share(2, 6, 7), share(2, 7, 8) + dx, share(2, 8, 10))))
    far = wide(to_z(narrow(share(2, 0, 2) + cx[:n] + cy[:n]), 2))
    bx = wide(
        to_x(
            narrow(
                share(1, 0, 1) + cy[n : n + h],
                share(1, 1, 2),
                share(1, 2, 3) + cy[n + h :],
                share(1, 3, 5),
            )
        )
    )
    by = wide(
        to_y(
            narrow(
                share(1, 5, 6),
                share(1, 6, 7) + cx[n : n + h],
                share(1, 7, 8),
                share(1, 8, 9) + cx[n + h :],
                share(1, 9, 10),
            )
        )
    )
    below = wide(to_z(narrow(share(0, 6, 8) + bx[:n] + by[:n]), 3))
    above = wide(to_z(narrow(share(0, 8, 10) + bx[n : 2 * n] + by[n : 2 * n]), 1))
    own_x = wide(to_x(narrow(share(0, 2, 3) + by[2 * n :], share(0, 3, 4))))
    own_y = wide(to_y(narrow(share(0, 4, 5), share(0, 5, 6) + bx[2 * n :])))
    others = lax.optimization_barrier(share(0, 0, 2) + below + above + far)
    return narrow(others + own_x + own_y)


def expert_kernel(plan, here_ref, *refs):
    planes, group_count, expert_count, width, top = plan
    counts = (12, 5, 3, 3) if planes else (1, 1, 3, 3)
    counts += (4, 4, 3) if planes else (1, 1, 3)
    parts, done = [], 0
    for count in counts:
        parts.append(refs[done : done + count])
        done += count
    own, other, (gate_hbm, up_hbm, down_hbm), _, own_out, other_out = parts[:6]
    gate_buf, up_buf, down_buf = parts[6]
    slots, select, scales, staged, sems, in_sems, out_sems, *room = refs[done:]
    sets = [[(ref, k) for ref in (gate_buf, up_buf, down_buf)] for k in range(gate_buf.shape[0])]
    if room:
        sets += [[(ref, k) for ref in room] for k in range(room[0].shape[0])]
    lanes = select.shape[2]
    half = lanes // 2
    piece = half // JOIN
    block = JOIN * CAP
    unit = piece // 2
    ahead, depth = gate_buf.shape[0], len(sets)

    def loads(e, slot):
        return [
            pltpu.make_async_copy(hbm.at[e], ref.at[k], sems.at[i, slot])
            for i, (hbm, (ref, k)) in enumerate(
                zip((gate_hbm, up_hbm, down_hbm), sets[slot], strict=True)
            )
        ]

    def slot_range(group):
        if planes:
            return slice(group * block, (group + 1) * block)
        return pl.ds(pl.multiple_of(group * block, block), block)

    def block_of(group):
        return pl.ds(pl.multiple_of(group * half, half), half)

    def takes(group):
        if not planes:
            return [
                pltpu.make_async_copy(
                    ref[0].at[block_of(group)],
                    staged.at[0, pl.ds(k * half, half)],
                    in_sems.at[k],
                )
                for k, ref in enumerate((own, other))
            ]
        copies, at = [], 0
        for side, where in ((own, TAKEN), (other, OTHER)):
            for b, f, t in where[group]:
                rows = (t - f) * unit
                copies.append(
                    pltpu.make_async_copy(
                        side[b].at[pl.ds(f * unit, rows)],
                        staged.at[group, pl.ds(at, rows)],
                        in_sems.at[len(copies) + 10 * group],
                    )
                )
                at += rows
        return copies

    def puts(group):
        if not planes:
            return [
                pltpu.make_async_copy(
                    staged.at[0, pl.ds(k * half, half), pl.ds(0, width)],
                    ref[0].at[block_of(group)],
                    out_sems.at[k],
                )
                for k, ref in enumerate((own_out, other_out))
            ]
        copies, at = [], 0
        for side in (own_out, other_out):
            for b, f, t in PLACES[group]:
                rows = (t - f) * unit
                copies.append(
                    pltpu.make_async_copy(
                        staged.at[group, pl.ds(at, rows), pl.ds(0, width)],
                        side[b].at[pl.ds(f * unit, rows)],
                        out_sems.at[len(copies) + 10 * group],
                    )
                )
                at += rows
        return copies

    def stage_of(group):
        return group if planes else 0

    def sort_rows(group):
        copies = takes(group)
        if not planes:
            for copy in copies:
                copy.start()
        for copy in copies:
            copy.wait()
        rows_ref = staged.at[stage_of(group)]
        first = here_ref[1]
        named = rows_ref[:, width:].astype(jnp.float32).T
        ids = named[:top]
        gates = named[top : 2 * top] + named[2 * top : 3 * top] + named[3 * top : 4 * top]
        earlier = lax.broadcasted_iota(jnp.int32, (lanes, lanes), 0)
        later = lax.broadcasted_iota(jnp.int32, (lanes, lanes), 1)
        same = ((earlier // piece) % JOIN) == ((later // piece) % JOIN)
        before = jnp.where(same & (earlier < later), 1.0, 0.0).astype(jnp.bfloat16)
        hits, gated = [], []
        for e in range(expert_count):
            hit = ids == (first + e).astype(jnp.float32)
            hits.append(jnp.sum(jnp.where(hit, 1.0, 0.0), axis=0, keepdims=True))
            gated.append(jnp.sum(jnp.where(hit, gates, 0.0), axis=0, keepdims=True))
        padded = hits + [jnp.zeros_like(hits[0])] * (-expert_count % 8)
        places = jnp.dot(
            jnp.concatenate(padded, axis=0).astype(jnp.bfloat16),
            before,
            preferred_element_type=jnp.float32,
        )
        slot = lax.broadcasted_iota(jnp.int32, (block, lanes), 0)
        lane = lax.broadcasted_iota(jnp.int32, (block, lanes), 1)
        fits = (slot // CAP) == ((lane // piece) % JOIN)
        place = (slot % CAP).astype(jnp.float32)
        at = slot_range(group)
        for e in range(expert_count):
            wanted = jnp.where(hits[e] > 0.5, places[e : e + 1], -1.0)
            picked = jnp.where(fits & (wanted == place), 1.0, 0.0)
            scale = jnp.sum(picked * gated[e], axis=1, keepdims=True)
            scales[e, at, :] = jnp.broadcast_to(scale, (block, 128))
            select[group, e * block : (e + 1) * block, :] = picked.astype(jnp.bfloat16)
        chosen = select[group]
        for c in range(0, width, COLS):
            columns = slice(c, c + COLS)
            sorted_rows = jnp.dot(
                chosen, rows_ref[:, columns], preferred_element_type=jnp.float32
            ).astype(jnp.bfloat16)
            for e in range(expert_count):
                slots[e, at, columns] = sorted_rows[e * block : (e + 1) * block]

    def run_expert(e, slot):
        copies = loads(e, slot)
        (gate_buf, k), (up_buf, _), (down_buf, _) = sets[slot]

        def arrived(copy):
            pl.when(e >= ahead)(copy.wait)

        def reload(i):
            @pl.when(e + depth < expert_count)
            def _():
                loads(e + depth, slot)[i].start()

        rows = slots[e]
        arrived(copies[0])
        gate = jnp.dot(rows, gate_buf[k], preferred_element_type=jnp.float32)
        reload(0)
        arrived(copies[1])
        up = jnp.dot(rows, up_buf[k], preferred_element_type=jnp.float32)
        reload(1)
        hidden = (gate / (1.0 + jnp.exp(-gate))) * up * scales[e][:, :1]
        hidden = hidden.astype(jnp.bfloat16)
        arrived(copies[2])
        for c in range(0, width, COLS):
            slots[e, :, c : c + COLS] = jnp.dot(
                hidden, down_buf[k, :, c : c + COLS], preferred_element_type=jnp.float32
            ).astype(jnp.bfloat16)

        reload(2)

    def run_experts(first):
        for slot in range(depth):
            run_expert(first * depth + slot, slot)

    def sum_rows(group):
        chosen = select[group]
        at = slot_range(group)
        for c in range(0, width, COLS):
            columns = slice(c, c + COLS)
            outs = jnp.concatenate([slots[e, at, columns] for e in range(expert_count)], axis=0)
            rows = lax.dot_general(
                chosen, outs, (((0,), (0,)), ((), ())), preferred_element_type=jnp.float32
            )
            staged[stage_of(group), :, columns] = rows.astype(jnp.bfloat16)
        for copy in puts(group):
            copy.start()
        if not planes:
            for copy in puts(group):
                copy.wait()

    def each(count, work):
        lax.fori_loop(0, count, lambda i, _: (work(i), 0)[1], 0)

    if planes:
        for group in range(group_count):
            for copy in takes(group):
                copy.start()
    for e in range(ahead, depth):
        for copy in loads(e, e):
            copy.start()
    if planes:
        for group in range(group_count):
            sort_rows(group)
    else:
        each(group_count, sort_rows)
    each(expert_count // depth, run_experts)
    if planes:
        for group in (2, 1, 3, 0):
            sum_rows(group)
        for group in (2, 1, 3, 0):
            for copy in puts(group):
                copy.wait()
    else:
        each(group_count, sum_rows)


def ahead_kernel(gate_hbm, up_hbm, down_hbm, _, __, gate_out, up_out, down_out, done_out, sems):
    copies = [
        pltpu.make_async_copy(hbm.at[e], out.at[e], sems.at[k, e])
        for e in range(gate_out.shape[0])
        for k, (hbm, out) in enumerate(
            ((gate_hbm, gate_out), (up_hbm, up_out), (down_hbm, down_out))
        )
    ]
    for copy in copies:
        copy.start()
    done_out[...] = jnp.zeros_like(done_out)
    for copy in copies:
        copy.wait()


def weights_ahead(gate_weight, up_weight, down_weight, *follows):
    depth = AHEAD if gate_weight.shape[0] % (AHEAD + MORE) == 0 else 1
    weights = [gate_weight, up_weight, down_weight]
    return pl.pallas_call(
        ahead_kernel,
        out_shape=[pltpu.VMEM((depth,) + w.shape[1:], w.dtype) for w in weights]
        + [jax.ShapeDtypeStruct(follows[0].shape, follows[0].dtype)],
        in_specs=[pl.BlockSpec(memory_space=pl.ANY)] * 5,
        out_specs=[pl.BlockSpec(memory_space=pltpu.VMEM)] * 4,
        scratch_shapes=[pltpu.SemaphoreType.DMA((3, depth))],
        compiler_params=pltpu.CompilerParams(vmem_limit_bytes=VMEM_LIMIT),
        cost_estimate=pl.CostEstimate(
            flops=0,
            bytes_accessed=sum(2 * depth * w[0].size for w in weights),
            transcendentals=0,
        ),
    )(*weights, *follows)


def expert_sums(own, other, top, owners, here, gate_weight, up_weight, down_weight, ahead):
    expert_count, width, hidden = gate_weight.shape
    planes = plane_of(owners)
    group_count = owners // JOIN
    half = sum(x.shape[0] for x in own) // group_count
    slot_rows = group_count * JOIN * CAP
    more = MORE if expert_count % (AHEAD + MORE) == 0 else 0
    depth = ahead[0].shape[0] + more
    ahead = [pltpu.with_memory_space_constraint(w, pltpu.VMEM) for w in ahead]
    if planes:
        out_rows = [u * half // 8 for u in BUNDLES] * 2
    else:
        out_rows = [own[0].shape[0]] * 2
    stages, copies = (group_count, 10 * group_count) if planes else (1, 2)
    weight_bytes = 3 * expert_count * width * hidden * 2
    sums = pl.pallas_call(
        functools.partial(expert_kernel, (planes, group_count, expert_count, width, top)),
        out_shape=[jax.ShapeDtypeStruct((r, width), jnp.bfloat16) for r in out_rows]
        + [pltpu.VMEM(w.shape, w.dtype) for w in ahead],
        input_output_aliases={
            1 + len(own) + len(other) + 3 + k: len(out_rows) + k for k in range(3)
        },
        in_specs=[pl.BlockSpec(memory_space=pltpu.SMEM)]
        + [pl.BlockSpec(memory_space=pl.ANY)] * (len(own) + len(other) + 3)
        + [pl.BlockSpec(memory_space=pltpu.VMEM)] * 3,
        out_specs=[pl.BlockSpec(memory_space=pl.ANY)] * len(out_rows)
        + [pl.BlockSpec(memory_space=pltpu.VMEM)] * 3,
        scratch_shapes=[
            pltpu.VMEM((expert_count, slot_rows, width), jnp.bfloat16),
            pltpu.VMEM((group_count, expert_count * JOIN * CAP, 2 * half), jnp.bfloat16),
            pltpu.VMEM((expert_count, slot_rows, 128), jnp.float32),
            pltpu.VMEM((stages, 2 * half, own[0].shape[1]), jnp.bfloat16),
            pltpu.SemaphoreType.DMA((3, depth)),
            pltpu.SemaphoreType.DMA((copies,)),
            pltpu.SemaphoreType.DMA((copies,)),
        ]
        + [pltpu.VMEM((more,) + w.shape[1:], w.dtype) for w in ahead if more],
        compiler_params=pltpu.CompilerParams(vmem_limit_bytes=VMEM_LIMIT),
        cost_estimate=pl.CostEstimate(
            flops=slot_rows * weight_bytes,
            bytes_accessed=weight_bytes,
            transcendentals=expert_count * slot_rows * hidden,
        ),
    )(here, *own, *other, gate_weight, up_weight, down_weight, *ahead)
    count = len(out_rows) // 2
    return sums[:count], sums[count : 2 * count]


def ask_kernel(here_ref, rows_hbm, routes_hbm, gates_hbm, own_ref, other_ref, routes, gates, asks, sems):
    width = rows_hbm.shape[1]
    half = rows_hbm.shape[0] // 2
    small = [
        pltpu.make_async_copy(routes_hbm, routes, sems.at[0]),
        pltpu.make_async_copy(gates_hbm, gates, sems.at[1]),
    ]
    large = [
        pltpu.make_async_copy(
            rows_hbm.at[pl.ds(pl.multiple_of(from_half * half, half), half)],
            ref.at[:, pl.ds(0, width)],
            sems.at[2 + k],
        )
        for k, (from_half, ref) in enumerate(
            ((here_ref[0], own_ref), (1 - here_ref[0], other_ref))
        )
    ]
    for copy in small + large:
        copy.start()
    for copy in small:
        copy.wait()
    terms = [routes[...].astype(jnp.float32)]
    left = gates[...]
    for _ in range(3):
        term = left.astype(jnp.bfloat16).astype(jnp.float32)
        terms.append(term)
        left = left - term
    blank = 128 - sum(t.shape[0] for t in terms)
    asked = jnp.concatenate(terms + [jnp.zeros((blank, 2 * half), jnp.float32)], axis=0).T
    asked = asked.astype(jnp.bfloat16)
    first, last = asked[:half], asked[half:]
    mine = here_ref[0] == 0
    own_ref[:, width:] = jnp.where(mine, first, last)
    asks[...] = jnp.where(mine, last, first)
    last = pltpu.make_async_copy(asks, other_ref.at[:, pl.ds(width, 128)], sems.at[4])
    last.start()
    for copy in large + [last]:
        copy.wait()


def ask(moe_rows, routes, route_gates, here):
    rows, width = moe_rows.shape
    half = jax.ShapeDtypeStruct((rows // 2, width + 128), jnp.bfloat16)
    return pl.pallas_call(
        ask_kernel,
        out_shape=(half, half),
        in_specs=[pl.BlockSpec(memory_space=pltpu.SMEM)]
        + [pl.BlockSpec(memory_space=pl.ANY)] * 3,
        out_specs=[pl.BlockSpec(memory_space=pltpu.VMEM), pl.BlockSpec(memory_space=pl.ANY)],
        scratch_shapes=[
            pltpu.VMEM(routes.shape[::-1], jnp.int32),
            pltpu.VMEM(routes.shape[::-1], jnp.float32),
            pltpu.VMEM((rows // 2, 128), jnp.bfloat16),
            pltpu.SemaphoreType.DMA((5,)),
        ],
        compiler_params=pltpu.CompilerParams(vmem_limit_bytes=4 * 1024 * 1024),
    )(
        here,
        *(pltpu.with_memory_space_constraint(x, pltpu.HBM) for x in (moe_rows, routes.T, route_gates.T)),
    )


def order_kernel(here_ref, own_ref, other_ref, out_ref):
    half = own_ref.shape[0]
    out_ref[pl.ds(pl.multiple_of(here_ref[0] * half, half), half)] = own_ref[...]
    out_ref[pl.ds(pl.multiple_of((1 - here_ref[0]) * half, half), half)] = other_ref[...]


def in_order(own, other, here):
    return pl.pallas_call(
        order_kernel,
        out_shape=jax.ShapeDtypeStruct((2 * own.shape[0], own.shape[1]), own.dtype),
        in_specs=[pl.BlockSpec(memory_space=pltpu.SMEM)]
        + [pl.BlockSpec(memory_space=pltpu.VMEM)] * 2,
        out_specs=pl.BlockSpec(memory_space=pltpu.VMEM),
        compiler_params=pltpu.CompilerParams(vmem_limit_bytes=4 * 1024 * 1024),
    )(here, own, other)


def route_rows(moe_rows, routes, route_gates, gate_weight, up_weight, down_weight, attend):
    owners = lax.axis_size("ep")
    top = routes.shape[1]
    core, chip = lax.axis_index("ctx"), lax.axis_index("ep")
    here = jnp.stack([core, chip * gate_weight.shape[0]]).astype(jnp.int32)

    def meanwhile(follows):
        packed, begun = attend(here, follows)
        *ahead, done = weights_ahead(gate_weight, up_weight, down_weight, follows, packed[0])
        return (ahead, packed), begun, done

    mine, theirs = ask(moe_rows, routes, route_gates, here)
    if plane_of(owners):
        own, other, (ahead, packed) = gather_rows(mine, meanwhile)
        other = [theirs] + other
    else:
        own = [lax.all_gather(mine, "ep", tiled=True)]
        other = [swap_ctx(own[0])]
        ahead, packed = meanwhile(mine)[0]
    own_sums, other_sums = expert_sums(
        own, other, top, owners, here, gate_weight, up_weight, down_weight, ahead
    )
    came = [None] * len(own_sums)
    for b in reversed(range(len(own_sums))):
        came[b] = swap_ctx(other_sums[b])
    if plane_of(owners):
        own_final = scatter_sums(own_sums, came)
    else:
        own_final = lax.psum_scatter(own_sums[0] + came[0], "ep", scatter_dimension=0, tiled=True)
    other_final = swap_ctx(own_final)
    return in_order(own_final, other_final, here), packed


def body(
    moe_rows,
    routes,
    route_gates,
    gate_weight,
    up_weight,
    down_weight,
    queries,
    latent_cache,
    cache_lengths,
):
    attend = functools.partial(attend_local, queries, latent_cache, cache_lengths)
    routed_output, packed = route_rows(
        moe_rows, routes, route_gates, gate_weight, up_weight, down_weight, attend
    )
    return (routed_output, join_cores(*packed))


def solution(mesh):
    in_specs = (
        P("ep", None),
        P("ep", None),
        P("ep", None),
        P("ep", None, "ctx"),
        P("ep", None, "ctx"),
        P("ep", "ctx", None),
        P("ep", None, None),
        P("ep", "ctx", None),
        P("ep"),
    )
    out_specs = (P("ep", None), P("ep", "ctx", None))
    return jax.shard_map(body, mesh=mesh, in_specs=in_specs, out_specs=out_specs, check_vma=False)
```

```python
import functools

import jax
import jax.numpy as jnp
from jax import lax
from jax.experimental import pallas as pl
from jax.experimental.pallas import tpu as pltpu
from jax.sharding import PartitionSpec as P

LAT = 512
CAP = 8
JOIN = 4
COLS = 512
AHEAD = 3
MORE = 1
VMEM_LIMIT = 55 * 512 * 1024

softmax_scale = 192.0 ** (-0.5)


def attend_kernel(request, here_ref, lengths_ref, queries_ref, cache_ref, kept_ref, sent_ref, zeros_ref, joined):
    zeros_ref[...] = jnp.zeros_like(zeros_ref)
    heads, span = queries_ref.shape[0], cache_ref.shape[1]
    share = heads // 2
    core = here_ref[0]
    scores = (
        jnp.dot(queries_ref[...], cache_ref[...], preferred_element_type=jnp.float32)
        * softmax_scale
    )
    positions = core * span + lax.broadcasted_iota(jnp.int32, (heads, span), 1)
    usable = positions < lengths_ref[request]
    masked = jnp.where(usable, scores, -1e30)
    top = jnp.max(masked, axis=1, keepdims=True)
    weights = jnp.where(usable, jnp.exp(masked - top), 0.0)
    total = jnp.sum(weights, axis=1, keepdims=True)
    joined[:, :LAT] = lax.dot_general(
        weights.astype(jnp.bfloat16),
        cache_ref[:LAT],
        (((1,), (1,)), ((), ())),
        preferred_element_type=jnp.float32,
    )
    lane = lax.broadcasted_iota(jnp.int32, (heads, 128), 1)
    joined[:, LAT:] = jnp.where(lane == 0, top, total)
    kept_ref[...] = joined[pl.ds(pl.multiple_of(core * share, share), share)]
    sent_ref[...] = joined[pl.ds(pl.multiple_of((1 - core) * share, share), share)]


def attend_part(queries, cache, lengths, request, here, like):
    heads, depth = queries.shape
    part = jax.ShapeDtypeStruct((heads // 2, LAT + 128), jnp.float32)
    return pl.pallas_call(
        functools.partial(attend_kernel, request),
        out_shape=(part, part, jax.ShapeDtypeStruct(like.shape, like.dtype)),
        in_specs=[pl.BlockSpec(memory_space=pltpu.SMEM)] * 2
        + [pl.BlockSpec(memory_space=pltpu.VMEM)] * 2,
        out_specs=(pl.BlockSpec(memory_space=pltpu.VMEM),) * 3,
        scratch_shapes=[pltpu.VMEM((heads, LAT + 128), jnp.float32)],
        compiler_params=pltpu.CompilerParams(vmem_limit_bytes=16 * 1024 * 1024),
        cost_estimate=pl.CostEstimate(
            flops=2 * heads * cache.shape[0] * (depth + LAT),
            bytes_accessed=cache.size * 2,
            transcendentals=heads * cache.shape[0],
        ),
    )(here, lengths, queries, cache.T)


def swap_ctx(x):
    return lax.ppermute(x, "ctx", [(0, 1), (1, 0)])


def attend_local(queries, latent_cache, cache_lengths, here, like):
    parts = [
        attend_part(queries[r], latent_cache[r], cache_lengths, r, here, like)
        for r in range(queries.shape[0])
    ]
    kept, sent, zeros = zip(*parts)
    return (jnp.stack(kept), jnp.stack(sent)), zeros[-1]


def join_cores(kept, sent):
    other = swap_ctx(sent)
    kept_top, other_top = kept[:, :, LAT : LAT + 1], other[:, :, LAT : LAT + 1]
    joined_top = jnp.maximum(kept_top, other_top)
    kept_factor = jnp.exp(kept_top - joined_top)
    other_factor = jnp.exp(other_top - joined_top)
    joined = kept * kept_factor + other * other_factor
    return (joined[:, :, :LAT] / joined[:, :, LAT + 1 : LAT + 2]).astype(jnp.bfloat16)


def plane_of(owners):
    return owners == 16


def send(x, target):
    count = lax.axis_size("ep")
    return lax.ppermute(x, "ep", [(i, target(i)) for i in range(count)])


def to_x(x):
    return send(x, lambda i: i ^ 1)


def to_y(x):
    return send(x, lambda i: i ^ 2)


def to_z(x, steps):
    return send(x, lambda i: (i + 4 * steps) % 16)


def cat(*pieces):
    return jnp.concatenate(pieces, axis=0)


def after(x, other):
    return lax.optimization_barrier((x, other))[0]


def gather_rows(rows, meanwhile):
    n = rows.shape[0]
    h = n // 2
    below, above = to_z(rows, 1), to_z(rows, 3)
    own_x, own_y = to_x(rows), to_y(rows)
    far = to_z(after(rows, below), 2)
    result, begun, done = meanwhile(above)
    bx = to_x(cat(below, above + begun, own_y[h:]))
    by = to_y(cat(below, above + begun, own_x[:h]))
    early = swap_ctx(cat(own_x, own_y, below, above))
    far = far + done
    cx = to_x(cat(far, by[h:n], by[n + h : 2 * n]))
    cy = to_y(cat(far, bx[:h], bx[n : n + h]))
    middle = swap_ctx(cat(bx, by, far))
    dx = to_x(cy[h:n])
    dy = to_y(cx[:h])
    late = swap_ctx(cat(cx, cy))
    own = [rows, own_x, own_y, below, above, bx, by, far, cx, cy, dx, dy]
    return own, [early, middle, late, swap_ctx(cat(dx, dy))], result


TAKEN = (
    ((0, 0, 2), (1, 0, 2), (2, 0, 2), (6, 4, 5), (5, 4, 5)),
    ((3, 0, 2), (5, 0, 2), (6, 0, 2), (9, 2, 3), (8, 2, 3)),
    ((7, 0, 2), (8, 0, 2), (9, 0, 2), (11, 0, 1), (10, 0, 1)),
    ((4, 0, 2), (5, 2, 4), (6, 2, 4), (9, 3, 4), (8, 3, 4)),
)
OTHER = (
    ((0, 0, 2), (1, 0, 2), (1, 2, 4), (2, 9, 10), (2, 4, 5)),
    ((1, 4, 6), (2, 0, 2), (2, 5, 7), (3, 6, 7), (3, 2, 3)),
    ((2, 10, 12), (3, 0, 2), (3, 4, 6), (4, 1, 2), (4, 0, 1)),
    ((1, 6, 8), (2, 2, 4), (2, 7, 9), (3, 7, 8), (3, 3, 4)),
)
PLACES = (
    ((0, 0, 2), (0, 2, 4), (0, 4, 6), (1, 9, 10), (1, 4, 5)),
    ((0, 6, 8), (1, 0, 2), (1, 5, 7), (2, 8, 9), (2, 4, 5)),
    ((2, 0, 2), (2, 2, 4), (2, 6, 8), (3, 1, 2), (3, 0, 1)),
    ((0, 8, 10), (1, 2, 4), (1, 7, 9), (2, 9, 10), (2, 5, 6)),
)
BUNDLES = (10, 10, 10, 2)


def scatter_sums(kept, came):
    n = kept[3].shape[0]
    h = n // 2

    def share(b, first, last):
        at = slice(first * h, last * h)
        return kept[b][at].astype(jnp.float32) + came[b][at].astype(jnp.float32)

    def wide(x):
        return x.astype(jnp.float32)

    def narrow(*pieces):
        return cat(*pieces).astype(jnp.bfloat16)

    dx = wide(to_x(narrow(share(3, 0, 1))))
    dy = wide(to_y(narrow(share(3, 1, 2))))
    cx = wide(to_x(narrow(share(2, 2, 3) + dy, share(2, 3, 6))))
    cy = wide(to_y(narrow(share(2, 6, 7), share(2, 7, 8) + dx, share(2, 8, 10))))
    far = wide(to_z(narrow(share(2, 0, 2) + cx[:n] + cy[:n]), 2))
    bx = wide(
        to_x(
            narrow(
                share(1, 0, 1) + cy[n : n + h],
                share(1, 1, 2),
                share(1, 2, 3) + cy[n + h :],
                share(1, 3, 5),
            )
        )
    )
    by = wide(
        to_y(
            narrow(
                share(1, 5, 6),
                share(1, 6, 7) + cx[n : n + h],
                share(1, 7, 8),
                share(1, 8, 9) + cx[n + h :],
                share(1, 9, 10),
            )
        )
    )
    below = wide(to_z(narrow(share(0, 6, 8) + bx[:n] + by[:n]), 3))
    above = wide(to_z(narrow(share(0, 8, 10) + bx[n : 2 * n] + by[n : 2 * n]), 1))
    own_x = wide(to_x(narrow(share(0, 2, 3) + by[2 * n :], share(0, 3, 4))))
    own_y = wide(to_y(narrow(share(0, 4, 5), share(0, 5, 6) + bx[2 * n :])))
    others = lax.optimization_barrier(share(0, 0, 2) + below + above + far)
    return narrow(others + own_x + own_y)


def expert_kernel(plan, here_ref, *refs):
    planes, group_count, expert_count, width, top = plan
    counts = (12, 5, 3, 3) if planes else (1, 1, 3, 3)
    counts += (4, 4, 3) if planes else (1, 1, 3)
    parts, done = [], 0
    for count in counts:
        parts.append(refs[done : done + count])
        done += count
    own, other, (gate_hbm, up_hbm, down_hbm), _, own_out, other_out = parts[:6]
    gate_buf, up_buf, down_buf = parts[6]
    slots, select, scales, staged, sems, in_sems, out_sems, *room = refs[done:]
    sets = [[(ref, k) for ref in (gate_buf, up_buf, down_buf)] for k in range(gate_buf.shape[0])]
    if room:
        sets += [[(ref, k) for ref in room] for k in range(room[0].shape[0])]
    lanes = select.shape[2]
    half = lanes // 2
    piece = half // JOIN
    block = JOIN * CAP
    unit = piece // 2
    ahead, depth = gate_buf.shape[0], len(sets)

    def loads(e, slot):
        return [
            pltpu.make_async_copy(hbm.at[e], ref.at[k], sems.at[i, slot])
            for i, (hbm, (ref, k)) in enumerate(
                zip((gate_hbm, up_hbm, down_hbm), sets[slot], strict=True)
            )
        ]

    def slot_range(group):
        if planes:
            return slice(group * block, (group + 1) * block)
        return pl.ds(pl.multiple_of(group * block, block), block)

    def block_of(group):
        return pl.ds(pl.multiple_of(group * half, half), half)

    def takes(group):
        if not planes:
            return [
                pltpu.make_async_copy(
                    ref[0].at[block_of(group)],
                    staged.at[0, pl.ds(k * half, half)],
                    in_sems.at[k],
                )
                for k, ref in enumerate((own, other))
            ]
        copies, at = [], 0
        for side, where in ((own, TAKEN), (other, OTHER)):
            for b, f, t in where[group]:
                rows = (t - f) * unit
                copies.append(
                    pltpu.make_async_copy(
                        side[b].at[pl.ds(f * unit, rows)],
                        staged.at[group, pl.ds(at, rows)],
                        in_sems.at[len(copies) + 10 * group],
                    )
                )
                at += rows
        return copies

    def puts(group):
        if not planes:
            return [
                pltpu.make_async_copy(
                    staged.at[0, pl.ds(k * half, half), pl.ds(0, width)],
                    ref[0].at[block_of(group)],
                    out_sems.at[k],
                )
                for k, ref in enumerate((own_out, other_out))
            ]
        copies, at = [], 0
        for side in (own_out, other_out):
            for b, f, t in PLACES[group]:
                rows = (t - f) * unit
                copies.append(
                    pltpu.make_async_copy(
                        staged.at[group, pl.ds(at, rows), pl.ds(0, width)],
                        side[b].at[pl.ds(f * unit, rows)],
                        out_sems.at[len(copies) + 10 * group],
                    )
                )
                at += rows
        return copies

    def stage_of(group):
        return group if planes else 0

    def sort_rows(group):
        copies = takes(group)
        if not planes:
            for copy in copies:
                copy.start()
        for copy in copies:
            copy.wait()
        rows_ref = staged.at[stage_of(group)]
        first = here_ref[1]
        named = rows_ref[:, width:].astype(jnp.float32).T
        ids = named[:top]
        gates = named[top : 2 * top] + named[2 * top : 3 * top] + named[3 * top : 4 * top]
        earlier = lax.broadcasted_iota(jnp.int32, (lanes, lanes), 0)
        later = lax.broadcasted_iota(jnp.int32, (lanes, lanes), 1)
        same = ((earlier // piece) % JOIN) == ((later // piece) % JOIN)
        before = jnp.where(same & (earlier < later), 1.0, 0.0).astype(jnp.bfloat16)
        hits, gated = [], []
        for e in range(expert_count):
            hit = ids == (first + e).astype(jnp.float32)
            hits.append(jnp.sum(jnp.where(hit, 1.0, 0.0), axis=0, keepdims=True))
            gated.append(jnp.sum(jnp.where(hit, gates, 0.0), axis=0, keepdims=True))
        padded = hits + [jnp.zeros_like(hits[0])] * (-expert_count % 8)
        places = jnp.dot(
            jnp.concatenate(padded, axis=0).astype(jnp.bfloat16),
            before,
            preferred_element_type=jnp.float32,
        )
        slot = lax.broadcasted_iota(jnp.int32, (block, lanes), 0)
        lane = lax.broadcasted_iota(jnp.int32, (block, lanes), 1)
        fits = (slot // CAP) == ((lane // piece) % JOIN)
        place = (slot % CAP).astype(jnp.float32)
        at = slot_range(group)
        for e in range(expert_count):
            wanted = jnp.where(hits[e] > 0.5, places[e : e + 1], -1.0)
            picked = jnp.where(fits & (wanted == place), 1.0, 0.0)
            scale = jnp.sum(picked * gated[e], axis=1, keepdims=True)
            scales[e, at, :] = jnp.broadcast_to(scale, (block, 128))
            select[group, e * block : (e + 1) * block, :] = picked.astype(jnp.bfloat16)
        chosen = select[group]
        for c in range(0, width, COLS):
            columns = slice(c, c + COLS)
            sorted_rows = jnp.dot(
                chosen, rows_ref[:, columns], preferred_element_type=jnp.float32
            ).astype(jnp.bfloat16)
            for e in range(expert_count):
                slots[e, at, columns] = sorted_rows[e * block : (e + 1) * block]

    def run_expert(e, slot):
        copies = loads(e, slot)
        (gate_buf, k), (up_buf, _), (down_buf, _) = sets[slot]

        def arrived(copy):
            pl.when(e >= ahead)(copy.wait)

        def reload(i):
            @pl.when(e + depth < expert_count)
            def _():
                loads(e + depth, slot)[i].start()

        rows = slots[e]
        arrived(copies[0])
        gate = jnp.dot(rows, gate_buf[k], preferred_element_type=jnp.float32)
        reload(0)
        arrived(copies[1])
        up = jnp.dot(rows, up_buf[k], preferred_element_type=jnp.float32)
        reload(1)
        hidden = (gate / (1.0 + jnp.exp(-gate))) * up * scales[e][:, :1]
        hidden = hidden.astype(jnp.bfloat16)
        arrived(copies[2])
        for c in range(0, width, COLS):
            slots[e, :, c : c + COLS] = jnp.dot(
                hidden, down_buf[k, :, c : c + COLS], preferred_element_type=jnp.float32
            ).astype(jnp.bfloat16)

        reload(2)

    def run_experts(first):
        for slot in range(depth):
            run_expert(first * depth + slot, slot)

    def sum_rows(group):
        chosen = select[group]
        at = slot_range(group)
        for c in range(0, width, COLS):
            columns = slice(c, c + COLS)
            outs = jnp.concatenate([slots[e, at, columns] for e in range(expert_count)], axis=0)
            rows = lax.dot_general(
                chosen, outs, (((0,), (0,)), ((), ())), preferred_element_type=jnp.float32
            )
            staged[stage_of(group), :, columns] = rows.astype(jnp.bfloat16)
        for copy in puts(group):
            copy.start()
        if not planes:
            for copy in puts(group):
                copy.wait()

    def each(count, work):
        lax.fori_loop(0, count, lambda i, _: (work(i), 0)[1], 0)

    if planes:
        for group in range(group_count):
            for copy in takes(group):
                copy.start()
    for e in range(ahead, depth):
        for copy in loads(e, e):
            copy.start()
    if planes:
        for group in range(group_count):
            sort_rows(group)
    else:
        each(group_count, sort_rows)
    each(expert_count // depth, run_experts)
    if planes:
        for group in (2, 1, 3, 0):
            sum_rows(group)
        for group in (2, 1, 3, 0):
            for copy in puts(group):
                copy.wait()
    else:
        each(group_count, sum_rows)


def ahead_kernel(gate_hbm, up_hbm, down_hbm, _, __, gate_out, up_out, down_out, done_out, sems):
    copies = [
        pltpu.make_async_copy(hbm.at[e], out.at[e], sems.at[k, e])
        for e in range(gate_out.shape[0])
        for k, (hbm, out) in enumerate(
            ((gate_hbm, gate_out), (up_hbm, up_out), (down_hbm, down_out))
        )
    ]
    for copy in copies:
        copy.start()
    done_out[...] = jnp.zeros_like(done_out)
    for copy in copies:
        copy.wait()


def weights_ahead(gate_weight, up_weight, down_weight, *follows):
    depth = AHEAD if gate_weight.shape[0] % (AHEAD + MORE) == 0 else 1
    weights = [gate_weight, up_weight, down_weight]
    return pl.pallas_call(
        ahead_kernel,
        out_shape=[pltpu.VMEM((depth,) + w.shape[1:], w.dtype) for w in weights]
        + [pltpu.VMEM(follows[0].shape, follows[0].dtype)],
        in_specs=[pl.BlockSpec(memory_space=pl.ANY)] * 5,
        out_specs=[pl.BlockSpec(memory_space=pltpu.VMEM)] * 4,
        scratch_shapes=[pltpu.SemaphoreType.DMA((3, depth))],
        compiler_params=pltpu.CompilerParams(vmem_limit_bytes=VMEM_LIMIT),
        cost_estimate=pl.CostEstimate(
            flops=0,
            bytes_accessed=sum(2 * depth * w[0].size for w in weights),
            transcendentals=0,
        ),
    )(*weights, *follows)


def expert_sums(own, other, top, owners, here, gate_weight, up_weight, down_weight, ahead):
    expert_count, width, hidden = gate_weight.shape
    planes = plane_of(owners)
    group_count = owners // JOIN
    half = sum(x.shape[0] for x in own) // group_count
    slot_rows = group_count * JOIN * CAP
    more = MORE if expert_count % (AHEAD + MORE) == 0 else 0
    depth = ahead[0].shape[0] + more
    ahead = [pltpu.with_memory_space_constraint(w, pltpu.VMEM) for w in ahead]
    if planes:
        out_rows = [u * half // 8 for u in BUNDLES] * 2
    else:
        out_rows = [own[0].shape[0]] * 2
    stages, copies = (group_count, 10 * group_count) if planes else (1, 2)
    kinds = [
        (pltpu.VMEM, pltpu.VMEM) if r < half else (jax.ShapeDtypeStruct, pl.ANY) for r in out_rows
    ]
    weight_bytes = 3 * expert_count * width * hidden * 2
    sums = pl.pallas_call(
        functools.partial(expert_kernel, (planes, group_count, expert_count, width, top)),
        out_shape=[out((r, width), jnp.bfloat16) for r, (out, _) in zip(out_rows, kinds)]
        + [pltpu.VMEM(w.shape, w.dtype) for w in ahead],
        input_output_aliases={
            1 + len(own) + len(other) + 3 + k: len(out_rows) + k for k in range(3)
        },
        in_specs=[pl.BlockSpec(memory_space=pltpu.SMEM)]
        + [pl.BlockSpec(memory_space=pl.ANY)] * (len(own) + len(other) + 3)
        + [pl.BlockSpec(memory_space=pltpu.VMEM)] * 3,
        out_specs=[pl.BlockSpec(memory_space=space) for _, space in kinds]
        + [pl.BlockSpec(memory_space=pltpu.VMEM)] * 3,
        scratch_shapes=[
            pltpu.VMEM((expert_count, slot_rows, width), jnp.bfloat16),
            pltpu.VMEM((group_count, expert_count * JOIN * CAP, 2 * half), jnp.bfloat16),
            pltpu.VMEM((expert_count, slot_rows, 128), jnp.float32),
            pltpu.VMEM((stages, 2 * half, own[0].shape[1]), jnp.bfloat16),
            pltpu.SemaphoreType.DMA((3, depth)),
            pltpu.SemaphoreType.DMA((copies,)),
            pltpu.SemaphoreType.DMA((copies,)),
        ]
        + [pltpu.VMEM((more,) + w.shape[1:], w.dtype) for w in ahead if more],
        compiler_params=pltpu.CompilerParams(vmem_limit_bytes=VMEM_LIMIT),
        cost_estimate=pl.CostEstimate(
            flops=slot_rows * weight_bytes,
            bytes_accessed=weight_bytes,
            transcendentals=expert_count * slot_rows * hidden,
        ),
    )(here, *own, *other, gate_weight, up_weight, down_weight, *ahead)
    count = len(out_rows) // 2
    return sums[:count], sums[count : 2 * count]


def ask_kernel(here_ref, rows_hbm, routes_hbm, gates_hbm, own_ref, other_ref, routes, gates, asks, sems):
    width = rows_hbm.shape[1]
    half = rows_hbm.shape[0] // 2
    small = [
        pltpu.make_async_copy(routes_hbm, routes, sems.at[0]),
        pltpu.make_async_copy(gates_hbm, gates, sems.at[1]),
    ]
    large = [
        pltpu.make_async_copy(
            rows_hbm.at[pl.ds(pl.multiple_of(from_half * half, half), half)],
            ref.at[:, pl.ds(0, width)],
            sems.at[2 + k],
        )
        for k, (from_half, ref) in enumerate(
            ((here_ref[0], own_ref), (1 - here_ref[0], other_ref))
        )
    ]
    for copy in small + large:
        copy.start()
    for copy in small:
        copy.wait()
    terms = [routes[...].astype(jnp.float32)]
    left = gates[...]
    for _ in range(3):
        term = left.astype(jnp.bfloat16).astype(jnp.float32)
        terms.append(term)
        left = left - term
    blank = 128 - sum(t.shape[0] for t in terms)
    asked = jnp.concatenate(terms + [jnp.zeros((blank, 2 * half), jnp.float32)], axis=0).T
    asked = asked.astype(jnp.bfloat16)
    first, last = asked[:half], asked[half:]
    mine = here_ref[0] == 0
    own_ref[:, width:] = jnp.where(mine, first, last)
    asks[...] = jnp.where(mine, last, first)
    last = pltpu.make_async_copy(asks, other_ref.at[:, pl.ds(width, 128)], sems.at[4])
    last.start()
    for copy in large + [last]:
        copy.wait()


def ask(moe_rows, routes, route_gates, here):
    rows, width = moe_rows.shape
    half = jax.ShapeDtypeStruct((rows // 2, width + 128), jnp.bfloat16)
    return pl.pallas_call(
        ask_kernel,
        out_shape=(half, half),
        in_specs=[pl.BlockSpec(memory_space=pltpu.SMEM)]
        + [pl.BlockSpec(memory_space=pl.ANY)] * 3,
        out_specs=[pl.BlockSpec(memory_space=pltpu.VMEM), pl.BlockSpec(memory_space=pl.ANY)],
        scratch_shapes=[
            pltpu.VMEM(routes.shape[::-1], jnp.int32),
            pltpu.VMEM(routes.shape[::-1], jnp.float32),
            pltpu.VMEM((rows // 2, 128), jnp.bfloat16),
            pltpu.SemaphoreType.DMA((5,)),
        ],
        compiler_params=pltpu.CompilerParams(vmem_limit_bytes=4 * 1024 * 1024),
    )(
        here,
        *(pltpu.with_memory_space_constraint(x, pltpu.HBM) for x in (moe_rows, routes.T, route_gates.T)),
    )


def order_kernel(here_ref, own_ref, other_ref, out_ref):
    half = own_ref.shape[0]
    out_ref[pl.ds(pl.multiple_of(here_ref[0] * half, half), half)] = own_ref[...]
    out_ref[pl.ds(pl.multiple_of((1 - here_ref[0]) * half, half), half)] = other_ref[...]


def in_order(own, other, here):
    return pl.pallas_call(
        order_kernel,
        out_shape=jax.ShapeDtypeStruct((2 * own.shape[0], own.shape[1]), own.dtype),
        in_specs=[pl.BlockSpec(memory_space=pltpu.SMEM)]
        + [pl.BlockSpec(memory_space=pltpu.VMEM)] * 2,
        out_specs=pl.BlockSpec(memory_space=pltpu.VMEM),
        compiler_params=pltpu.CompilerParams(vmem_limit_bytes=4 * 1024 * 1024),
    )(here, own, other)


def route_rows(moe_rows, routes, route_gates, gate_weight, up_weight, down_weight, attend):
    owners = lax.axis_size("ep")
    top = routes.shape[1]
    core, chip = lax.axis_index("ctx"), lax.axis_index("ep")
    here = jnp.stack([core, chip * gate_weight.shape[0]]).astype(jnp.int32)

    def meanwhile(follows):
        packed, begun = attend(here, follows)
        *ahead, done = weights_ahead(gate_weight, up_weight, down_weight, follows, packed[0])
        return (ahead, packed), begun, done

    mine, theirs = ask(moe_rows, routes, route_gates, here)
    if plane_of(owners):
        own, other, (ahead, packed) = gather_rows(mine, meanwhile)
        other = [theirs] + other
    else:
        own = [lax.all_gather(mine, "ep", tiled=True)]
        other = [swap_ctx(own[0])]
        ahead, packed = meanwhile(mine)[0]
    own_sums, other_sums = expert_sums(
        own, other, top, owners, here, gate_weight, up_weight, down_weight, ahead
    )
    came = [None] * len(own_sums)
    for b in reversed(range(len(own_sums))):
        came[b] = swap_ctx(other_sums[b])
    if plane_of(owners):
        own_final = scatter_sums(own_sums, came)
    else:
        own_final = lax.psum_scatter(own_sums[0] + came[0], "ep", scatter_dimension=0, tiled=True)
    other_final = swap_ctx(own_final)
    return in_order(own_final, other_final, here), packed


def body(
    moe_rows,
    routes,
    route_gates,
    gate_weight,
    up_weight,
    down_weight,
    queries,
    latent_cache,
    cache_lengths,
):
    attend = functools.partial(attend_local, queries, latent_cache, cache_lengths)
    routed_output, packed = route_rows(
        moe_rows, routes, route_gates, gate_weight, up_weight, down_weight, attend
    )
    return (routed_output, join_cores(*packed))


def solution(mesh):
    in_specs = (
        P("ep", None),
        P("ep", None),
        P("ep", None),
        P("ep", None, "ctx"),
        P("ep", None, "ctx"),
        P("ep", "ctx", None),
        P("ep", None, None),
        P("ep", "ctx", None),
        P("ep"),
    )
    out_specs = (P("ep", None), P("ep", "ctx", None))
    return jax.shard_map(body, mesh=mesh, in_specs=in_specs, out_specs=out_specs, check_vma=False)
```
